32 devices in a mesh: sub: 4 (over z), inner: 8 (over y, x, core).
Axes of the slice: x: 2, y: 2, z: 4, core: 2. Of those that a mesh axis runs over, the one named last changes fastest.
Arguments:
- front_leaf: bfloat16 [20480, 1024], P(('sub', 'inner')), may hold values from -6 to 6
- front_mid: bfloat16 [20480, 1024], P(('sub', 'inner')), may hold values from -6 to 6
- front_top: bfloat16 [20480, 1024], P(('sub', 'inner')), may hold values from -6 to 6
- dinv_leaf: bfloat16 [2048, 256], P('sub'), may hold values from -0.046875 to 0.046875
- dinv_mid: bfloat16 [1024, 256], P('sub'), may hold values from -0.046875 to 0.046875
- dinv_top: bfloat16 [512, 256], P('sub'), may hold values from -0.046875 to 0.046875
- live_rows: int32 [3, 32], P(None, ('sub', 'inner')), may hold values from 320 to 640, as said below
- map_leaf: int32 [20480], P(('sub', 'inner')), may hold values from 0 to 1279, as said below
- map_mid: int32 [20480], P(('sub', 'inner')), may hold values from 0 to 1279, as said below
Outputs:
- contribution: bfloat16 [20480, 512], P(('sub', 'inner'))
The draws below stay inside these ranges and needn't reach their ends.
Inputs may be any that keep to these rules, and one draw needn't show every extreme that they name: `live_rows`: at each level some device block has all 640 rows live. `map_leaf`: within each block of 640 consecutive entries the codes are distinct and exactly half of them are 640 or more. `map_mid`: within each block of 640 consecutive entries the codes are distinct and exactly half of them are 640 or more.
All inputs are finite; a program needn't handle non-finite values.
Results may differ from the reference program's by a relative error of at most 0.0065.
Values may be sent and summed in bfloat16 or wider, within the bound.
No kernel may reach another device: no remote copies, remote signals or barrier semaphores. Data moves between devices by JAX's collectives and lax.ppermute only.
A program may use at most 64 MiB of HBM per device.

```python
import jax
import jax.numpy as jnp
from jax import lax

ROWS = 640
PANEL = 512
BLOCK = 256
NEXT = 512
TOTAL = 20480
N_SUB = 4
N_INNER = 8


def draw_live_rows(key, part):
    block_total = N_SUB * N_INNER
    counts = jax.random.randint(key, (3, block_total), ROWS // 2, ROWS + 1)
    max_spots = jax.random.randint(jax.random.fold_in(key, 7), (3,), 0, block_total)
    return counts.at[jnp.arange(3), max_spots].set(ROWS).astype(jnp.int32)


def shared_codes(key):
    block_total = N_SUB * N_INNER
    block_keys = jax.random.split(key, block_total)

    def one_block(block_key):
        own_key, far_key, mix_key = jax.random.split(block_key, 3)
        own_part = jax.random.permutation(own_key, ROWS)[:ROWS // 2]
        far_part = jax.random.permutation(far_key, ROWS)[:ROWS // 2] + ROWS
        return jax.random.permutation(mix_key, jnp.concatenate([own_part, far_part]))
    return jax.vmap(one_block)(block_keys).reshape(block_total * ROWS).astype(jnp.int32)


def draw_map_leaf(key, part):
    return shared_codes(jax.random.fold_in(key, 11))


def draw_map_mid(key, part):
    return shared_codes(jax.random.fold_in(key, 13))


def block_scale(key, dims, cuts, least, largest):
    gain, own = 1.0, jax.random.fold_in(key, 6)
    for position, blocks in cuts:
        draws = jnp.exp(jax.random.uniform(jax.random.fold_in(own, position), (blocks,), jnp.float32, least / len(cuts), largest / len(cuts)))
        gain = gain * jnp.repeat(draws, dims[position] // blocks).reshape([-1 if axis == position else 1 for axis in range(len(dims))])
    return gain


def noise(stream_key, dims, deviation, reach, pieces=(), held_as=jnp.bfloat16):
    values = jax.random.normal(stream_key, dims, jnp.float32) * deviation
    if len(pieces) > 0:
        values = block_scale(stream_key, dims, pieces, -0.22, 0.18) * values
    return jnp.clip(values, min=-reach, max=reach).astype(held_as)


def setup_inputs(seed: int = 0) -> dict:
    streams_of = jax.random.split(jax.random.key(seed), 10)
    return {
        "front_leaf": noise(streams_of[0], (TOTAL, PANEL + NEXT), 1.0, 6.0, ((0, 32),)),
        "front_mid": noise(streams_of[1], (TOTAL, PANEL + NEXT), 1.0, 6.0, ((0, 32),)),
        "front_top": noise(streams_of[2], (TOTAL, PANEL + NEXT), 1.0, 6.0, ((0, 32),)),
        "dinv_leaf": noise(streams_of[3], (N_SUB * PANEL, BLOCK), (3 * BLOCK * PANEL ** 0.5) ** -0.5, 0.046875, ((0, 4),)),
        "dinv_mid": noise(streams_of[4], (N_SUB // 2 * PANEL, BLOCK), (3 * BLOCK * PANEL ** 0.5) ** -0.5, 0.046875, ((0, 4),)),
        "dinv_top": noise(streams_of[5], (N_SUB // 4 * PANEL, BLOCK), (3 * BLOCK * PANEL ** 0.5) ** -0.5, 0.046875, ((0, 4),)),
        "live_rows": draw_live_rows(jax.random.fold_in(streams_of[9], 71), 0),
        "map_leaf": draw_map_leaf(jax.random.fold_in(streams_of[9], 71), 0),
        "map_mid": draw_map_mid(jax.random.fold_in(streams_of[9], 71), 0),
    }


def level_update(front_whole, inverse, live_count, level_index):
    groups = N_SUB >> level_index
    group_rows = (N_INNER << level_index) * ROWS
    block_count = PANEL // BLOCK
    pivot_count = NEXT // (N_INNER << level_index)
    row_mask = (lax.broadcasted_iota(jnp.int32, (N_SUB * N_INNER, ROWS), 1) < live_count[:, None]).reshape(groups, group_rows)

    def one_group(items):
        front_part, inv_part, mask_part = items
        panel_part = front_part[:, :PANEL].astype(jnp.float32).reshape(group_rows, block_count, BLOCK)
        inv_table = inv_part.astype(jnp.float32).reshape(block_count, BLOCK, BLOCK)
        factor = jnp.einsum("rbk,bjk->rbj", panel_part, inv_table).reshape(group_rows, PANEL)
        factor = jnp.where(mask_part[:, None], factor, 0.0).astype(jnp.bfloat16)
        pivots = factor.reshape(group_rows // ROWS, ROWS, PANEL)[:, :pivot_count].reshape(NEXT, PANEL)
        product = jnp.dot(factor, pivots.T, preferred_element_type=jnp.float32)
        update = jnp.where(mask_part[:, None], front_part[:, PANEL:].astype(jnp.float32) - product, 0.0)
        return update.astype(jnp.bfloat16)

    result = lax.map(one_group, (front_whole.reshape(groups, group_rows, PANEL + NEXT), inverse.reshape(groups, PANEL, BLOCK), row_mask))
    return result.reshape(groups * group_rows, NEXT)


def extend_add(update, code_map, parent, level_index):
    total_rows = update.shape[0]
    row_ids = lax.iota(jnp.int32, total_rows)
    block_ids = row_ids // ROWS
    sub_ids = block_ids // N_INNER
    inner_ids = block_ids % N_INNER
    outward = code_map >= ROWS
    target_sub = jnp.where(outward, jnp.bitwise_xor(sub_ids, 1 << level_index), sub_ids)
    target_row = jnp.where(outward, code_map - ROWS, code_map)
    destination = ((target_sub * N_INNER + inner_ids) * ROWS + target_row).astype(jnp.int32)
    merged = parent[:, :NEXT].astype(jnp.float32).at[destination].add(update.astype(jnp.float32))
    return jnp.concatenate([merged.astype(jnp.bfloat16), parent[:, NEXT:]], 1)


def reference(front_leaf, front_mid, front_top, dinv_leaf, dinv_mid, dinv_top, live_rows, map_leaf, map_mid):
    update = level_update(front_leaf, dinv_leaf, live_rows[0], 0)
    parent = extend_add(update, map_leaf, front_mid, 0)
    update = level_update(parent, dinv_mid, live_rows[1], 1)
    parent = extend_add(update, map_mid, front_top, 1)
    return level_update(parent, dinv_top, live_rows[2], 2)
```

```python
import jax
import jax.numpy as jnp
from jax import lax
from jax.experimental import pallas as pl
from jax.experimental.pallas import tpu as pltpu
from jax.sharding import PartitionSpec as P

BF = jnp.bfloat16
F32 = jnp.float32
NT = (((1,), (1,)), ((), ()))
NN = (((1,), (0,)), ((), ()))


def dot(a, b, dims):
    return lax.dot_general(a, b, dims, preferred_element_type=F32)


def swap(value, axis, mask):
    return lax.ppermute(value, axis, [(i, i ^ mask) for i in range(lax.axis_size(axis))])


def call(body, out_shape, smem=(), n_in=0, name=None):
    vm = pl.BlockSpec(memory_space=pltpu.VMEM)
    sm = pl.BlockSpec(memory_space=pltpu.SMEM)
    specs = [sm if i in smem else vm for i in range(n_in)]
    outs = [jax.ShapeDtypeStruct(s, d) for s, d in out_shape]
    return pl.pallas_call(
        body, in_specs=specs, out_specs=[vm] * len(outs), out_shape=outs, name=name,
        compiler_params=pltpu.CompilerParams(vmem_limit_bytes=50 * 1024 * 1024),
    )


def one_hot(row, count, offset=0):
    ids = lax.broadcasted_iota(jnp.int32, (count, row.shape[1]), 0) + offset
    return jnp.where(ids == row, 1.0, 0.0).astype(BF)


def slots_of(code, rows):
    outward = code >= rows
    flags = jnp.broadcast_to(jnp.where(outward, 1.0, 0.0).astype(BF), (8, rows))
    a = lax.broadcasted_iota(jnp.int32, (rows, rows), 0)
    b = lax.broadcasted_iota(jnp.int32, (rows, rows), 1)
    upper = jnp.where(a < b, 1.0, 0.0).astype(BF)
    rank = dot(flags, upper, NN)[:1].astype(jnp.int32)
    return jnp.where(outward, rank, -1)


def prep_body(map0, map0_far, map1, map1_far, slot0, target0, slot1, target1):
    rows = map0.shape[1]
    for own, far, slot, target in (
        (map0, map0_far, slot0, target0),
        (map1, map1_far, slot1, target1),
    ):
        slot[...] = slots_of(own[...], rows)
        far_code = far[...]
        pick = one_hot(slots_of(far_code, rows), rows // 2)
        row = far_code - rows
        high = row >> 8
        low = row & 255
        high_row = dot(jnp.broadcast_to(high.astype(F32).astype(BF), (8, rows)), pick, NT)[:1]
        low_row = dot(jnp.broadcast_to(low.astype(F32).astype(BF), (8, rows)), pick, NT)[:1]
        target[...] = high_row.astype(jnp.int32) * 256 + low_row.astype(jnp.int32)


def scaled(panel, inverse):
    block = inverse.shape[1]
    parts = [
        dot(panel[:, b * block:(b + 1) * block], inverse[b * block:(b + 1) * block], NT)
        for b in range(inverse.shape[0] // block)
    ]
    return jnp.concatenate(parts, 1)


def reordered(value, outer, middle):
    rows = value.shape[0]
    part = rows // (outer * middle)
    if middle == 1:
        return value
    if part % 16 == 0:
        return jnp.concatenate(
            [value[(o * middle + m) * part:(o * middle + m + 1) * part]
             for m in range(middle) for o in range(outer)], 0)
    target = lax.broadcasted_iota(jnp.int32, (rows, rows), 0)
    source = lax.broadcasted_iota(jnp.int32, (rows, rows), 1)
    k = target % part
    o = target // part % outer
    m = target // (part * outer)
    return dot(jnp.where((o * middle + m) * part + k == source, 1.0, 0.0).astype(BF), value, NN).astype(BF)


def level_math(panel, rest, gathered, inverse, live, middle, inner):
    rows = panel.shape[0]
    mask = lax.broadcasted_iota(jnp.int32, (rows, 1), 0) < live
    factor = jnp.where(mask, scaled(panel, inverse), 0.0).astype(BF)
    pivots = reordered(scaled(gathered, inverse).astype(BF), inner, middle)
    product = dot(factor, pivots, NT)
    return jnp.where(mask, rest.astype(F32) - product, 0.0).astype(BF)


def sends(update, code, slot, pivot_out, bulk_out):
    rows = update.shape[0]
    n = pivot_out.shape[0] // 2
    pick = jnp.concatenate([one_hot(code, n), one_hot(code, n, rows)], 0) if n % 16 == 0 else None
    if pick is None:
        ids = lax.broadcasted_iota(jnp.int32, (2 * n, rows), 0)
        pick = jnp.where(jnp.where(ids < n, ids, ids - n + rows) == code, 1.0, 0.0).astype(BF)
    pivot_out[...] = dot(pick, update, NN).astype(BF)
    bulk_out[...] = dot(one_hot(slot, bulk_out.shape[0]), update, NN).astype(BF)


def merged_own(update, code, parent):
    return parent.astype(F32) + dot(one_hot(code, update.shape[0]), update, NN)


def per_device(front_leaf, front_mid, front_top, dinv_leaf, dinv_mid, dinv_top, live_rows, map_leaf, map_mid):
    rows = front_leaf.shape[0]
    panel = dinv_leaf.shape[0]
    cols = front_leaf.shape[1] - panel
    inner = lax.axis_size("inner")
    half = rows // 2
    n = [cols // (inner << l) for l in range(3)]
    sub = lax.axis_index("sub")
    low0 = sub & 1 == 0
    low1 = sub & 2 == 0

    def pair(mine, other, low):
        return jnp.where(low, jnp.concatenate([mine, other], 0), jnp.concatenate([other, mine], 0))

    code0 = map_leaf.reshape(1, rows)
    code1 = map_mid.reshape(1, rows)
    raw0 = lax.all_gather(front_leaf[:n[0], :panel], "inner", axis=0, tiled=True)
    far0 = swap(code0, "sub", 1)
    far1 = swap(code1, "sub", 2)
    mid_other = swap(dinv_mid, "sub", 1)
    top_other = swap(dinv_top, "sub", 1)
    inv_mid = pair(dinv_mid, mid_other, low0)
    top_pair = pair(dinv_top, top_other, low0)
    inv_top = pair(top_pair, swap(top_pair, "sub", 2), low1)
    mid_head = front_mid[:n[1], :panel]
    top_head = front_top[:n[2], :panel]
    mid_heads = pair(mid_head, swap(mid_head, "sub", 1), low0)
    top_heads = pair(top_head, swap(top_head, "sub", 1), low0)
    top_heads = pair(top_heads, swap(top_heads, "sub", 2), low1)
    slot0, target0, slot1, target1 = call(
        prep_body, [((1, rows), jnp.int32), ((1, half), jnp.int32)] * 2, n_in=4, name="prep"
    )(code0, far0, code1, far1)

    def level0(live, front, gathered, inverse, code, slot, update_out, pivot_out, bulk_out):
        update = level_math(front[:, :panel], front[:, panel:], gathered[...], inverse[...], live[0, 0], 1, inner)
        update_out[...] = update
        sends(update, code[...], slot[...], pivot_out, bulk_out)

    update0, pivot0, bulk0 = call(
        level0, [((rows, cols), BF), ((2 * n[1], cols), BF), ((half, cols), BF)], smem=(0,), n_in=6, name="level0"
    )(live_rows, front_leaf, raw0, dinv_leaf, code0, slot0)
    pivot0_other = swap(pivot0, "sub", 1)
    bulk0_other = swap(bulk0, "sub", 1)

    def own(update, code, parent, out):
        out[...] = merged_own(update[...], code[...], parent[:, :cols])

    merged0, = call(own, [((rows, cols), F32)], n_in=3, name="own0")(update0, code0, front_mid)
    own_sum = pivot0[:n[1]].astype(F32) + pivot0_other[n[1]:].astype(F32)
    far_sum = pivot0_other[:n[1]].astype(F32) + pivot0[n[1]:].astype(F32)
    raw1 = (mid_heads.astype(F32) + pair(own_sum, far_sum, low0)).astype(BF)
    raw1 = lax.all_gather(raw1, "inner", axis=0, tiled=True)

    def level1(live, front, merged, got, target, gathered, inverse, code, slot, update_out, pivot_out, bulk_out):
        landing = lax.broadcasted_iota(jnp.int32, (rows, half), 0) == target[...]
        assembled = (merged[...] + dot(jnp.where(landing, 1.0, 0.0).astype(BF), got[...], NN)).astype(BF)
        update = level_math(assembled, front[:, panel:], gathered[...], inverse[...], live[1, 0], 2, inner)
        update_out[...] = update
        sends(update, code[...], slot[...], pivot_out, bulk_out)

    update1, pivot1, bulk1 = call(
        level1, [((rows, cols), BF), ((2 * n[2], cols), BF), ((half, cols), BF)], smem=(0,), n_in=9, name="level1"
    )(live_rows, front_mid, merged0, bulk0_other, target0, raw1, inv_mid, code1, slot1)
    pivot1_z = [pivot1] + [swap(pivot1, "sub", m) for m in (1, 2, 3)]
    bulk1_other = swap(bulk1, "sub", 2)
    merged1, = call(own, [((rows, cols), F32)], n_in=3, name="own1")(update1, code1, front_top)
    sums = []
    for m in range(4):
        sums.append(pivot1_z[m][:n[2]].astype(F32) + pivot1_z[m ^ 2][n[2]:].astype(F32))
    raw2 = pair(pair(sums[0], sums[1], low0), pair(sums[2], sums[3], low0), low1)
    raw2 = (top_heads.astype(F32) + raw2).astype(BF)
    raw2 = lax.all_gather(raw2, "inner", axis=0, tiled=True)

    def level2(live, front, merged, got, target, gathered, inverse, out):
        landing = lax.broadcasted_iota(jnp.int32, (rows, half), 0) == target[...]
        assembled = (merged[...] + dot(jnp.where(landing, 1.0, 0.0).astype(BF), got[...], NN)).astype(BF)
        out[...] = level_math(assembled, front[:, panel:], gathered[...], inverse[...], live[2, 0], 4, inner)

    out, = call(level2, [((rows, cols), BF)], smem=(0,), n_in=7, name="level2")(
        live_rows, front_top, merged1, bulk1_other, target1, raw2, inv_top
    )
    return out


def solution(mesh):
    row = P(("sub", "inner"), None)
    placed = (
        row, row, row, P("sub", None), P("sub", None), P("sub", None),
        P(None, ("sub", "inner")), P(("sub", "inner")), P(("sub", "inner")),
    )
    return jax.shard_map(per_device, mesh=mesh, in_specs=placed, out_specs=row, check_vma=False)
```

```python
import jax
import jax.numpy as jnp
from jax import lax
from jax.experimental import pallas as pl
from jax.experimental.pallas import tpu as pltpu
from jax.sharding import PartitionSpec as P


BF = jnp.bfloat16
F32 = jnp.float32
I32 = jnp.int32
NT = (((1,), (1,)), ((), ()))
NN = (((1,), (0,)), ((), ()))
VM = pl.BlockSpec(memory_space=pltpu.VMEM)
SM = pl.BlockSpec(memory_space=pltpu.SMEM)
AN = pl.BlockSpec(memory_space=pltpu.HBM)


def dot(a, b, dims):
    return lax.dot_general(a, b, dims, preferred_element_type=F32)


def swap(value, axis, mask):
    return lax.ppermute(value, axis, [(i, i ^ mask) for i in range(lax.axis_size(axis))])


def later(value, *others):
    return lax.optimization_barrier((value,) + others)[0]


def call(body, in_specs, outs, scratch=(), out_specs=None):
    made = pl.pallas_call(
        body, in_specs=in_specs, out_specs=out_specs or [VM] * len(outs),
        out_shape=[jax.ShapeDtypeStruct(s, d) for s, d in outs], scratch_shapes=scratch,
        compiler_params=pltpu.CompilerParams(vmem_limit_bytes=16 * 1024 * 1024),
    )

    def run(*args):
        return made(*[
            pltpu.with_memory_space_constraint(a, pltpu.HBM) if spec is AN else a
            for a, spec in zip(args, in_specs)
        ])

    return run


def copies(sems, pairs):
    made = [pltpu.make_async_copy(a, b, sems.at[i]) for i, (a, b) in enumerate(pairs)]
    for c in made:
        c.start()
    return made


def one_hot(row, count):
    ids = lax.broadcasted_iota(I32, (count, row.shape[1]), 0)
    return jnp.where(ids == row, 1.0, 0.0).astype(BF)


def slots_of(code, rows):
    outward = code >= rows
    flags = jnp.broadcast_to(jnp.where(outward, 1.0, 0.0).astype(BF), (8, rows))
    a = lax.broadcasted_iota(I32, (rows, rows), 0)
    b = lax.broadcasted_iota(I32, (rows, rows), 1)
    upper = jnp.where(a < b, 1.0, 0.0).astype(BF)
    rank = dot(flags, upper, NN)[:1].astype(I32)
    return jnp.where(outward, rank, -1)


def landing_of(code, rows):
    pick = one_hot(slots_of(code, rows), rows // 2)
    target = one_hot(code - rows, rows)
    return dot(target, pick, NT).astype(BF)


def row_picks(code, live, n):
    rows = code.shape[1]
    alive = lax.broadcasted_iota(I32, (1, rows), 1) < live
    shown = jnp.where(alive, code, -1)
    slot = jnp.where(alive, slots_of(code, rows), -1)
    ids = lax.broadcasted_iota(I32, (2 * n, rows), 0)
    pivot = jnp.where(jnp.where(ids < n, ids, ids + (rows - n)) == shown, 1.0, 0.0).astype(BF)
    bulk = one_hot(slot, rows // 2)
    return jnp.concatenate([pivot, bulk], 0)


def own_pick(code, live):
    rows = code.shape[1]
    return one_hot(jnp.where(lax.broadcasted_iota(I32, (1, rows), 1) < live, code, -1), rows)


def scaled(panel, inverse):
    block = inverse.shape[1]
    parts = [
        dot(panel[:, b * block:(b + 1) * block], inverse[b * block:(b + 1) * block], NT)
        for b in range(inverse.shape[0] // block)
    ]
    return jnp.concatenate(parts, 1)


def factor_of(panel, inverse, live):
    mask = lax.broadcasted_iota(I32, (panel.shape[0], 1), 0) < live
    return jnp.where(mask, scaled(panel, inverse), 0.0).astype(BF)


def reordered(value, outer, middle):
    rows = value.shape[0]
    part = rows // (outer * middle)
    if middle == 1:
        return value
    if part % 16 == 0:
        return jnp.concatenate(
            [value[(o * middle + m) * part:(o * middle + m + 1) * part]
             for m in range(middle) for o in range(outer)], 0)
    target = lax.broadcasted_iota(I32, (rows, rows), 0)
    source = lax.broadcasted_iota(I32, (rows, rows), 1)
    k = target % part
    o = target // part % outer
    m = target // (part * outer)
    return dot(jnp.where((o * middle + m) * part + k == source, 1.0, 0.0).astype(BF), value, NN).astype(BF)


def spread(block):
    if lax.axis_size("inner") != 8 or block.shape[0] % 64:
        return {}
    return {m: swap(block, "inner", m) for m in GATHER_ORDER}


def collect(block, got, *before):
    if not got:
        return [lax.all_gather(block, "inner", axis=0, tiled=True)]
    got = dict(got)
    got[0] = block
    got[1] = swap(block, "inner", 1)
    for m in GATHER_ORDER:
        got[m] = later(got[m], *before)
        got[m + 1] = swap(got[m], "inner", 1)
    return [got[m] for m in range(8)]


GATHER_ORDER = (6, 4, 2)


def pivots_from(blocks, inverse, pivots, middle, inner):
    if len(blocks) == 1:
        pivots[...] = reordered(scaled(blocks[0][...], inverse[...]).astype(BF), inner, middle)
        return
    size = blocks[0].shape[0]
    part = size // middle
    made = scaled(jnp.concatenate([block[...] for block in blocks], 0), inverse[...]).astype(BF)
    for m in range(len(blocks)):
        at = (lax.axis_index("inner") ^ m) * part
        for q in range(middle):
            pivots[pl.ds(pl.multiple_of(q * part * inner + at, part), part), :] = (
                made[m * size + q * part:m * size + (q + 1) * part])


def code_row(ref):
    return jnp.concatenate([ref[i:i + 1] for i in range(ref.shape[0])], 1)


def up16(count):
    return (count + 15) // 16 * 16


def per_device(front_leaf, front_mid, front_top, dinv_leaf, dinv_mid, dinv_top, live_rows, map_leaf, map_mid):
    rows = front_leaf.shape[0]
    panel, block = dinv_leaf.shape
    cols = front_leaf.shape[1] - panel
    inner = lax.axis_size("inner")
    half = rows // 2
    n = [cols // (inner << l) for l in range(3)]

    lanes = 128 if rows % 128 == 0 else rows
    code0 = map_leaf.reshape(rows // lanes, lanes)
    code1 = map_mid.reshape(rows // lanes, lanes)
    live = live_rows.reshape(1, 3)

    mr, tr = dinv_mid.shape[0] // 2, dinv_top.shape[0] // 2
    at_top, at_code, at_mid = 0, tr + up16(n[2]), tr + up16(n[2]) + 16
    small = (tr + up16(n[2]) + 16, panel)
    large = (small[0] + mr + up16(n[1]), panel)

    def pack(code0_ref, code1_ref, mid, top, fmid, ftop, leaf, near, wide, c0v, c1v, head, sems):
        made = []
        for out in (near, wide):
            made += [
                (top.at[:tr], out.at[at_top:at_top + tr, :block]),
                (top.at[tr:], out.at[at_top:at_top + tr, block:]),
                (ftop.at[:n[2], :panel], out.at[tr:tr + n[2]]),
            ]
        made += [
            (mid.at[:mr], near.at[at_mid:at_mid + mr, :block]),
            (mid.at[mr:], near.at[at_mid:at_mid + mr, block:]),
            (fmid.at[:n[1], :panel], near.at[at_mid + mr:at_mid + mr + n[1]]),
        ]
        made = copies(sems, [(code0_ref, c0v), (code1_ref, c1v)] + made + [(leaf.at[:n[0], :panel], head)])
        made[0].wait()
        made[1].wait()
        code = jnp.concatenate([code_row(c0v), code_row(c1v)], 0)
        parts = jnp.concatenate([code >> 8, code & 255, jnp.zeros((4, rows), I32)], 0)
        parts = parts.astype(F32).astype(BF)
        padded = jnp.concatenate([parts, jnp.zeros((8, 2 * panel - rows), BF)], 1)
        packed = jnp.concatenate([padded[:, :panel], padded[:, panel:]], 0)
        near[at_code:at_code + 16] = packed
        wide[at_code:at_code + 16] = packed
        for c in made[2:]:
            c.wait()

    near, wide, code0, code1, block0 = call(
        pack, [AN] * 7,
        [(large, BF), (small, BF), (code0.shape, I32), (code1.shape, I32), ((n[0], panel), BF)],
        scratch=[pltpu.SemaphoreType.DMA((12,))],
    )(code0, code1, dinv_mid, dinv_top, front_mid, front_top, front_leaf)
    got0 = spread(block0)
    near_1 = swap(near, "sub", 1)
    wide_2 = swap(wide, "sub", 2)
    wide_3 = swap(wide, "sub", 3)

    def sent(level):
        return [((2 * n[level] + half, cols), BF)] * 2

    def before0(live_ref, code, front_ref, inverse, mid, fs, cs, factor, iv, front, mid_v, sems):
        made = copies(sems, [(inverse, iv), (front_ref, front), (mid, mid_v)])
        pick = row_picks(code_row(code), live_ref[0, 0], n[1])
        made[0].wait()
        made[1].wait()
        factor[...] = factor_of(front[:, :panel], iv[...], live_ref[0, 0])
        cs[...] = dot(pick, front[:, panel:], NN).astype(BF)
        fs[...] = dot(pick, factor[...], NN).astype(BF)
        made[2].wait()

    fs0, cs0, factor0, inv_leaf, leaf, mid = call(
        before0, [SM, VM, AN, AN, AN],
        sent(1) + [((rows, panel), BF), (dinv_leaf.shape, BF), (front_leaf.shape, BF), (front_mid.shape, BF)],
        scratch=[pltpu.SemaphoreType.DMA((3,))],
    )(live, code0, front_leaf, dinv_leaf, front_mid)
    blocks0 = collect(block0, got0, fs0)

    def chain(middle):
        def body(fs, cs, inverse, *refs):
            blocks, (pivots, out, bulk) = refs[:-3], refs[-3:]
            pivots_from(blocks, inverse, pivots, middle, inner)
            update = (cs[...].astype(F32) - dot(fs[...], pivots[...], NT)).astype(BF)
            out[...] = update[:out.shape[0]]
            bulk[...] = update[out.shape[0]:]

        return body

    def after(level, fs, cs, inverse, blocks):
        return call(
            chain(1 << level), [VM] * (3 + len(blocks)),
            [((cols, panel), BF), ((2 * n[level + 1], cols), BF), ((half, cols), BF)],
        )(fs, cs, inverse, *blocks)

    def own(level, code, factor, front, pivots, parent):
        def body(live_ref, code_ref, factor_ref, front_ref, pivots_ref, parent_ref, out):
            update = (front_ref[:, panel:].astype(F32) - dot(factor_ref[...], pivots_ref[...], NT)).astype(BF)
            pick = own_pick(code_row(code_ref), live_ref[0, level])
            out[...] = parent_ref[:, :cols].astype(F32) + dot(pick, update, NN)

        return call(body, [SM] + [VM] * 5, [((rows, cols), F32)])(
            live, code, factor, front, pivots, parent)[0]

    pivots0, pivot0, bulk0 = after(0, fs0, cs0, inv_leaf, blocks0)
    pivot0_other = swap(pivot0, "sub", 1)
    bulk0_other = swap(bulk0, "sub", 1)

    def landing_from(src, row, out):
        packed = src[at_code:at_code + 16].astype(F32).astype(I32)
        high = jnp.concatenate([packed[row:row + 1], packed[row + 8:row + 9]], 1)[:, :rows]
        low = jnp.concatenate([packed[row + 2:row + 3], packed[row + 10:row + 11]], 1)[:, :rows]
        out[...] = landing_of(high * 256 + low, rows)

    def unpack1(mine, near_ref, inv_mid, heads1, land0):
        sub = lax.axis_index("sub")
        for q, src in enumerate((mine, near_ref)):
            at = ((sub & 1) ^ q) * 2 * mr
            inv_mid[pl.ds(pl.multiple_of(at, mr), mr), :] = src[at_mid:at_mid + mr, :block]
            inv_mid[pl.ds(pl.multiple_of(at + mr, mr), mr), :] = src[at_mid:at_mid + mr, block:]
            heads1[q] = src[at_mid + mr:at_mid + mr + up16(n[1])]
        landing_from(near_ref, 0, land0)

    def unpack2(mine, near_ref, wide2, wide3, inv_top, heads2, land1):
        sub = lax.axis_index("sub")
        for q, src in enumerate((mine, near_ref, wide2, wide3)):
            at = ((sub & 3) ^ q) * 2 * tr
            inv_top[pl.ds(pl.multiple_of(at, tr), tr), :] = src[at_top:at_top + tr, :block]
            inv_top[pl.ds(pl.multiple_of(at + tr, tr), tr), :] = src[at_top:at_top + tr, block:]
            heads2[q] = src[tr:tr + up16(n[2])]
        landing_from(wide2, 1, land1)

    inv_mid, heads1, land0 = call(
        unpack1, [VM] * 2, [(dinv_leaf.shape, BF), ((2, up16(n[1]), panel), BF), ((rows, half), BF)],
    )(near, later(near_1, pivot0))

    def early1(live_ref, code, front, top_ref, pick_out, cs, top_v, sems):
        made, = copies(sems, [(top_ref, top_v)])
        pick = row_picks(code_row(code), live_ref[0, 1], n[2])
        pick_out[...] = pick
        cs[...] = dot(pick, front[:, panel:], NN).astype(BF)
        made.wait()

    pick1, cs1, top = call(
        early1, [SM, VM, VM, AN], [((2 * n[2] + half, rows), BF)] + sent(2)[:1] + [(front_top.shape, BF)],
        scratch=[pltpu.SemaphoreType.DMA((1,))],
    )(live, later(code1, pivot0), mid, front_top)

    def raised(count, flip):
        def body(heads, *refs):
            others, out = refs[:-1], refs[-1]
            sub = lax.axis_index("sub")
            made = []
            for q in range(len(others)):
                total = others[q][:count].astype(F32) + others[q ^ flip][count:].astype(F32)
                made.append(heads[q][:count].astype(F32) + total)
            bit = 1
            while len(made) > 1:
                low = (sub & bit) == 0
                made = [
                    jnp.concatenate([jnp.where(low, a, b), jnp.where(low, b, a)], 0)
                    for a, b in zip(made[::2], made[1::2])
                ]
                bit *= 2
            out[...] = made[0].astype(BF)

        return body

    raw1, = call(raised(n[1], 1), [VM] * 3, [((2 * n[1], panel), BF)])(later(heads1, pick1), pivot0, pivot0_other)
    spread1 = spread(raw1)
    merged0 = own(0, code0, factor0, leaf, pivots0, mid)

    def before1(live_ref, pick, merged, got, land, inverse, fs, factor):
        assembled = (merged[...] + dot(land[...], got[...], NN)).astype(BF)
        factor[...] = factor_of(assembled, inverse[...], live_ref[0, 1])
        fs[...] = dot(pick[...], factor[...], NN).astype(BF)

    fs1, factor1 = call(
        before1, [SM] + [VM] * 5, sent(2)[:1] + [((rows, panel), BF)],
    )(live, pick1, merged0, bulk0_other, land0, inv_mid)
    blocks1 = collect(raw1, spread1, fs1)
    pivots1, pivot1, bulk1 = after(1, fs1, cs1, inv_mid, blocks1)
    others = [pivot1] + [swap(pivot1, "sub", m) for m in (1, 2, 3)]
    bulk1_other = swap(bulk1, "sub", 2)
    inv_top, heads2, land1 = call(
        unpack2, [VM] * 4,
        [(dinv_leaf.shape, BF), ((4, up16(n[2]), panel), BF), ((rows, half), BF)],
    )(near, near_1, wide_2, later(wide_3, pivot1))
    raw2, = call(raised(n[2], 2), [VM] * 5, [((4 * n[2], panel), BF)])(heads2, *others)
    spread2 = spread(raw2)
    merged1 = own(1, code1, factor1, mid, pivots1, top)
    blocks2 = collect(raw2, spread2, merged1)

    def last_pivots(inverse, *refs):
        pivots_from(refs[:-1], inverse, refs[-1], 4, inner)

    pivots2, = call(last_pivots, [VM] * (1 + len(blocks2)), [((cols, panel), BF)])(inv_top, *blocks2)

    steps = 2 if rows % 32 == 0 else 1
    part = rows // steps

    def level2(live_ref, front, merged, got, land, inverse, pivots, out, ov, sems):
        assembled = (merged[...] + dot(land[...], got[...], NN)).astype(BF)
        factor = factor_of(assembled, inverse[...], live_ref[0, 2])
        mask = lax.broadcasted_iota(I32, (rows, 1), 0) < live_ref[0, 2]
        writes = []
        for i in range(steps):
            at = slice(i * part, (i + 1) * part)
            product = dot(factor[at], pivots[...], NT)
            ov[at] = jnp.where(mask[at], front[at, panel:].astype(F32) - product, 0.0).astype(BF)
            writes += copies(sems.at[i:i + 1], [(ov.at[at], out.at[at])])
        for write in writes:
            write.wait()

    out, = call(
        level2, [SM] + [VM] * 6, [((rows, cols), BF)],
        scratch=[pltpu.VMEM((rows, cols), BF), pltpu.SemaphoreType.DMA((steps,))],
        out_specs=[AN],
    )(live, top, merged1, bulk1_other, land1, inv_top, pivots2)
    return out


def solution(mesh):
    row = P(("sub", "inner"), None)
    placed = (
        row, row, row, P("sub", None), P("sub", None), P("sub", None),
        P(None, ("sub", "inner")), P(("sub", "inner")), P(("sub", "inner")),
    )

    return jax.shard_map(per_device, mesh=mesh, in_specs=placed, out_specs=row, check_vma=False)
```

```python
import jax
import jax.numpy as jnp
from jax import lax
from jax.experimental import pallas as pl
from jax.experimental.pallas import tpu as pltpu
from jax.sharding import PartitionSpec as P


BF = jnp.bfloat16
F32 = jnp.float32
I32 = jnp.int32
NT = (((1,), (1,)), ((), ()))
NN = (((1,), (0,)), ((), ()))
VM = pl.BlockSpec(memory_space=pltpu.VMEM)
SM = pl.BlockSpec(memory_space=pltpu.SMEM)
VP = pl.BlockSpec(memory_space=pltpu.VMEM)
AN = pl.BlockSpec(memory_space=pltpu.HBM)


def dot(a, b, dims):
    return lax.dot_general(a, b, dims, preferred_element_type=F32)


def swap(value, axis, mask):
    return lax.ppermute(value, axis, [(i, i ^ mask) for i in range(lax.axis_size(axis))])


def later(value, *others):
    return lax.optimization_barrier((value,) + others)[0]


def call(body, in_specs, outs, scratch=(), out_specs=None):
    made = pl.pallas_call(
        body, in_specs=in_specs, out_specs=out_specs or [VM] * len(outs),
        out_shape=[jax.ShapeDtypeStruct(s, d) for s, d in outs], scratch_shapes=scratch,
        compiler_params=pltpu.CompilerParams(vmem_limit_bytes=16 * 1024 * 1024),
    )

    def run(*args):
        return made(*[
            pltpu.with_memory_space_constraint(a, pltpu.HBM) if spec is AN
            else pltpu.with_memory_space_constraint(a, pltpu.VMEM) if spec is VP else a
            for a, spec in zip(args, in_specs)
        ])

    return run


def copies(sems, pairs):
    made = [pltpu.make_async_copy(a, b, sems.at[i]) for i, (a, b) in enumerate(pairs)]
    for c in made:
        c.start()
    return made


def one_hot(row, count):
    ids = lax.broadcasted_iota(I32, (count, row.shape[1]), 0)
    return jnp.where(ids == row, 1.0, 0.0).astype(BF)


def slots_of(code, rows):
    outward = code >= rows
    flags = jnp.broadcast_to(jnp.where(outward, 1.0, 0.0).astype(BF), (8, rows))
    a = lax.broadcasted_iota(I32, (rows, rows), 0)
    b = lax.broadcasted_iota(I32, (rows, rows), 1)
    upper = jnp.where(a < b, 1.0, 0.0).astype(BF)
    rank = dot(flags, upper, NN)[:1].astype(I32)
    return jnp.where(outward, rank, -1)


def landing_of(code, rows):
    pick = one_hot(slots_of(code, rows), rows // 2)
    target = one_hot(code - rows, rows)
    return dot(target, pick, NT).astype(BF)


def row_picks(code, live, n):
    rows = code.shape[1]
    alive = lax.broadcasted_iota(I32, (1, rows), 1) < live
    shown = jnp.where(alive, code, -1)
    slot = jnp.where(alive, slots_of(code, rows), -1)
    ids = lax.broadcasted_iota(I32, (2 * n, rows), 0)
    pivot = jnp.where(jnp.where(ids < n, ids, ids + (rows - n)) == shown, 1.0, 0.0).astype(BF)
    bulk = one_hot(slot, rows // 2)
    return jnp.concatenate([pivot, bulk], 0)


def own_pick(code, live):
    rows = code.shape[1]
    return one_hot(jnp.where(lax.broadcasted_iota(I32, (1, rows), 1) < live, code, -1), rows)


def scaled(panel, inverse):
    block = inverse.shape[1]
    parts = [
        dot(panel[:, b * block:(b + 1) * block], inverse[b * block:(b + 1) * block], NT)
        for b in range(inverse.shape[0] // block)
    ]
    return jnp.concatenate(parts, 1)


def factor_of(panel, inverse, live):
    mask = lax.broadcasted_iota(I32, (panel.shape[0], 1), 0) < live
    return jnp.where(mask, scaled(panel, inverse), 0.0).astype(BF)


def reordered(value, outer, middle):
    rows = value.shape[0]
    part = rows // (outer * middle)
    if middle == 1:
        return value
    if part % 16 == 0:
        return jnp.concatenate(
            [value[(o * middle + m) * part:(o * middle + m + 1) * part]
             for m in range(middle) for o in range(outer)], 0)
    target = lax.broadcasted_iota(I32, (rows, rows), 0)
    source = lax.broadcasted_iota(I32, (rows, rows), 1)
    k = target % part
    o = target // part % outer
    m = target // (part * outer)
    return dot(jnp.where((o * middle + m) * part + k == source, 1.0, 0.0).astype(BF), value, NN).astype(BF)


def spread(block):
    if lax.axis_size("inner") != 8 or block.shape[0] % 32:
        return {}
    return {m: swap(block, "inner", m) for m in GATHER_ORDER}


def collect(block, got):
    if not got:
        return [lax.all_gather(block, "inner", axis=0, tiled=True)]
    got = dict(got)
    got[0] = block
    for m in (0,) + GATHER_ORDER:
        got[m + 1] = swap(got[m], "inner", 1)
    return [got[m] for m in range(8)]


GATHER_ORDER = (6, 4, 2)


def pivots_from(blocks, inverse, pivots, middle, inner):
    if len(blocks) == 1:
        pivots[...] = reordered(scaled(blocks[0], inverse).astype(BF), inner, middle)
        return
    size = blocks[0].shape[0]
    part = size // middle
    made = scaled(jnp.concatenate(blocks, 0), inverse).astype(BF)
    for m in range(len(blocks)):
        at = (lax.axis_index("inner") ^ m) * part
        for q in range(middle):
            pivots[pl.ds(pl.multiple_of(q * part * inner + at, part), part), :] = (
                made[m * size + q * part:m * size + (q + 1) * part])


def up16(count):
    return (count + 15) // 16 * 16


def code_row(ref):
    return jnp.concatenate([ref[i:i + 1] for i in range(ref.shape[0])], 1)


def up16(count):
    return (count + 15) // 16 * 16


def per_device(front_leaf, front_mid, front_top, dinv_leaf, dinv_mid, dinv_top, live_rows, map_leaf, map_mid):
    rows = front_leaf.shape[0]
    panel, block = dinv_leaf.shape
    cols = front_leaf.shape[1] - panel
    inner = lax.axis_size("inner")
    half = rows // 2
    n = [cols // (inner << l) for l in range(3)]

    lanes = 128 if rows % 128 == 0 else rows
    code0 = map_leaf.reshape(rows // lanes, lanes)
    code1 = map_mid.reshape(rows // lanes, lanes)
    live = live_rows.reshape(1, 3)

    mr = dinv_mid.shape[0] // 2
    share = dinv_top.shape[0] // inner
    shared = inner == 8 and share % 16 == 0 and lanes == 128 and rows // lanes <= share and 2 * block == panel

    def pack(code0_ref, code1_ref, mid, fmid, ftop, leaf, near, c0v, c1v, head, top_head, sems):
        made = copies(sems, [
            (code0_ref, c0v), (code1_ref, c1v), (leaf.at[:n[0], :panel], head),
            (mid.at[:mr], near.at[:mr, :block]), (mid.at[mr:], near.at[:mr, block:]),
            (fmid.at[:n[1], :panel], near.at[mr + 16:mr + 16 + n[1]]), (ftop.at[:n[2], :panel], top_head),
        ])
        made[0].wait()
        code = code_row(c0v)
        parts = jnp.concatenate([code >> 8, code & 255, jnp.zeros((6, rows), I32)], 0).astype(F32).astype(BF)
        padded = jnp.concatenate([parts, jnp.zeros((8, 2 * panel - rows), BF)], 1)
        near[mr:mr + 16] = jnp.concatenate([padded[:, :panel], padded[:, panel:]], 0)
        for c in made[1:]:
            c.wait()

    near, code0, code1, block0, top_head = call(
        pack, [AN] * 6,
        [((mr + 16 + up16(n[1]), panel), BF), (code0.shape, I32), (code1.shape, I32), ((n[0], panel), BF),
         ((n[2], panel), BF)],
        scratch=[pltpu.SemaphoreType.DMA((7,))],
    )(code0, code1, dinv_mid, front_mid, front_top, front_leaf)
    got0 = spread(block0)
    near_1 = swap(near, "sub", 1)

    def sent(level):
        return [((2 * n[level] + half, cols), BF)] * 2

    def before0(live_ref, code, front, inverse, fs, cs, factor):
        pick = row_picks(code_row(code), live_ref[0, 0], n[1])
        factor[...] = factor_of(front[:, :panel], inverse[...], live_ref[0, 0])
        cs[...] = dot(pick, front[:, panel:], NN).astype(BF)
        fs[...] = dot(pick, factor[...], NN).astype(BF)

    fs0, cs0, factor0 = call(
        before0, [SM, VM, VP, VP], sent(1) + [((rows, panel), BF)],
    )(live, code0, front_leaf, dinv_leaf)
    blocks0 = collect(block0, got0)

    def chain(middle, count, headed, extra):
        def body(fs, cs, inverse, *refs):
            refs = list(refs)
            head = refs.pop(0) if headed else None
            code_ref, top = (refs.pop(0), refs.pop(0)) if extra else (None, None)
            blocks, (pivots, out, bulk) = refs[:-3], refs[-3:]
            pivots_from([ref[...] for ref in blocks], inverse[...], pivots, middle, inner)
            update = (cs[...].astype(F32) - dot(fs[...], pivots[...], NT)).astype(BF)
            out[:count] = (update[:count].astype(F32) + head[...].astype(F32)).astype(BF) if headed else update[:count]
            out[count:2 * count] = update[count:2 * count]
            if extra:
                tail = slice(2 * count, 2 * count + share)
                at = pl.multiple_of(lax.axis_index("inner") * share, share)
                out[tail, :block] = top[pl.ds(at, share), :]
                code = jnp.concatenate([code_ref[...], jnp.zeros((share - rows // lanes, lanes), I32)], 0)
                out[tail, block:block + lanes] = (code >> 8).astype(F32).astype(BF)
                out[tail, block + lanes:] = (code & 255).astype(F32).astype(BF)
            bulk[...] = update[2 * count:]

        return body

    def after(level, fs, cs, inverse, blocks, head=(), extra=()):
        count = n[level + 1]
        return call(
            chain(1 << level, count, bool(head), bool(extra)),
            [VM] * (3 + len(head) + len(extra) + len(blocks)),
            [((cols, panel), BF), ((2 * count + (share if extra else 0), cols), BF), ((half, cols), BF)],
        )(fs, cs, inverse, *head, *extra, *blocks)

    def own(level, code, factor, front, pivots, parent):
        def body(live_ref, code_ref, factor_ref, front_ref, pivots_ref, parent_ref, out):
            update = (front_ref[:, panel:].astype(F32) - dot(factor_ref[...], pivots_ref[...], NT)).astype(BF)
            pick = own_pick(code_row(code_ref), live_ref[0, level])
            out[...] = parent_ref[:, :cols].astype(F32) + dot(pick, update, NN)

        return call(body, [SM, VM, VM, VP, VM, VP], [((rows, cols), F32)])(
            live, code, factor, front, pivots, parent)[0]

    pivots0, pivot0, bulk0 = after(0, fs0, cs0, dinv_leaf, blocks0)
    pivot0_other = swap(pivot0, "sub", 1)
    bulk0_other = swap(bulk0, "sub", 1)

    def unpack1(mine, near_ref, inv_mid, heads1, land0):
        sub = lax.axis_index("sub")
        for q, src in enumerate((mine, near_ref)):
            at = ((sub & 1) ^ q) * 2 * mr
            inv_mid[pl.ds(pl.multiple_of(at, mr), mr), :] = src[:mr, :block]
            inv_mid[pl.ds(pl.multiple_of(at + mr, mr), mr), :] = src[:mr, block:]
            heads1[q] = src[mr + 16:]
        packed = near_ref[mr:mr + 16].astype(F32).astype(I32)
        high = jnp.concatenate([packed[0:1], packed[8:9]], 1)[:, :rows]
        low = jnp.concatenate([packed[1:2], packed[9:10]], 1)[:, :rows]
        land0[...] = landing_of(high * 256 + low, rows)

    inv_mid, heads1, land0 = call(
        unpack1, [VM] * 2,
        [(dinv_leaf.shape, BF), ((2, up16(n[1]), panel), BF), ((rows, half), BF)],
    )(near, later(near_1, pivot0))

    def early1(live_ref, code, front, pick_out, cs):
        pick = row_picks(code_row(code), live_ref[0, 1], n[2])
        pick_out[...] = pick
        cs[...] = dot(pick, front[:, panel:], NN).astype(BF)

    pick1, cs1 = call(
        early1, [SM, VM, VP], [((2 * n[2] + half, rows), BF)] + sent(2)[:1],
    )(live, later(code1, pivot0), front_mid)

    def raised(count, flip, headed, extra):
        def body(*refs):
            heads, others, out = refs[0] if headed else None, refs[headed:-1], refs[-1]
            sub = lax.axis_index("sub")

            def ordered(made):
                bit = 1
                while len(made) > 1:
                    low = (sub & bit) == 0
                    made = [
                        jnp.concatenate([jnp.where(low, a, b), jnp.where(low, b, a)], 0)
                        for a, b in zip(made[::2], made[1::2])
                    ]
                    bit *= 2
                return made[0]

            made = [
                others[q][:count].astype(F32) + others[q ^ flip][count:2 * count].astype(F32)
                for q in range(len(others))
            ]
            if headed:
                made = [heads[q][:count].astype(F32) + part for q, part in enumerate(made)]
            total = ordered(made)
            size = total.shape[0]
            out[:size] = total.astype(BF)
            if extra:
                tops = ordered([ref[2 * count:2 * count + share, :block].astype(F32) for ref in others]).astype(BF)
                for q in range(len(others)):
                    at = size + q // 2 * share
                    lane = q % 2 * block
                    out[at:at + share, lane:lane + block] = tops[q * share:(q + 1) * share]

        return body

    raw1, = call(raised(n[1], 1, 1, False), [VM] * 3, [((2 * n[1], panel), BF)])(
        later(heads1, pick1), pivot0, pivot0_other)
    spread1 = spread(raw1)
    merged0 = own(0, code0, factor0, front_leaf, pivots0, front_mid)

    def before1(live_ref, pick, merged, got, land, inverse, fs, factor):
        assembled = (merged[...] + dot(land[...], got[...], NN)).astype(BF)
        factor[...] = factor_of(assembled, inverse[...], live_ref[0, 1])
        fs[...] = dot(pick[...], factor[...], NN).astype(BF)

    fs1, factor1 = call(
        before1, [SM] + [VM] * 5, sent(2)[:1] + [((rows, panel), BF)],
    )(live, pick1, merged0, bulk0_other, land0, inv_mid)
    blocks1 = collect(raw1, spread1)
    pivots1, pivot1, bulk1 = after(
        1, fs1, cs1, inv_mid, blocks1, (top_head,), (code1, dinv_top) if shared else ())
    others = [pivot1] + [swap(pivot1, "sub", m) for m in (1, 2, 3)]
    bulk1_other = swap(bulk1, "sub", 2)
    raw2, = call(raised(n[2], 2, 0, shared), [VM] * 4, [((4 * n[2] + (2 * share if shared else 0), panel), BF)])(*others)
    spread2 = spread(raw2)
    merged1 = own(1, code1, factor1, front_mid, pivots1, front_top)
    blocks2 = collect(raw2, spread2)

    def landing1(src, land1):
        if not shared:
            land1[...] = landing_of(code_row(src), rows)
            return
        packed = src[2 * n[2]:, block:].astype(F32).astype(I32)
        code = packed[:rows // lanes, :lanes] * 256 + packed[:rows // lanes, lanes:]
        land1[...] = landing_of(jnp.concatenate([code[i:i + 1] for i in range(rows // lanes)], 1), rows)

    far1 = others[2] if shared else swap(code1, "sub", 2)
    land1, = call(landing1, [VM], [((rows, half), BF)])(later(far1, raw2))

    if shared:
        def last_pivots(*refs):
            blocks, pivots, inv_top = refs[:-2], refs[-2], refs[-1]
            size = 4 * n[2]
            for m, ref in enumerate(blocks):
                for q in range(4):
                    at = q * inner * share + (lax.axis_index("inner") ^ m) * share
                    row, lane = size + q // 2 * share, q % 2 * block
                    inv_top[pl.ds(pl.multiple_of(at, share), share), :] = ref[row:row + share, lane:lane + block]
            pivots_from([ref[:size] for ref in blocks], inv_top[...], pivots, 4, inner)

        pivots2, inv_top = call(
            last_pivots, [VM] * len(blocks2), [((cols, panel), BF), (dinv_leaf.shape, BF)])(*blocks2)
    else:
        def last_pivots(inverse, *refs):
            pivots_from([ref[...] for ref in refs[:-1]], inverse[...], refs[-1], 4, inner)

        sub = lax.axis_index("sub")
        inv_top = dinv_top
        for bit in (1, 2):
            other = swap(inv_top, "sub", bit)
            inv_top = jnp.where(
                sub & bit == 0, jnp.concatenate([inv_top, other], 0), jnp.concatenate([other, inv_top], 0))
        pivots2, = call(last_pivots, [VM] * (1 + len(blocks2)), [((cols, panel), BF)])(inv_top, *blocks2)

    steps = 2 if rows % 32 == 0 else 1
    part = rows // steps

    def level2(live_ref, front, merged, got, land, inverse, pivots, out, ov, sems):
        assembled = (merged[...] + dot(land[...], got[...], NN)).astype(BF)
        factor = factor_of(assembled, inverse[...], live_ref[0, 2])
        mask = lax.broadcasted_iota(I32, (rows, 1), 0) < live_ref[0, 2]
        writes = []
        for i in range(steps):
            at = slice(i * part, (i + 1) * part)
            product = dot(factor[at], pivots[...], NT)
            ov[at] = jnp.where(mask[at], front[at, panel:].astype(F32) - product, 0.0).astype(BF)
            writes += copies(sems.at[i:i + 1], [(ov.at[at], out.at[at])])
        for write in writes:
            write.wait()

    out, = call(
        level2, [SM, VP] + [VM] * 5, [((rows, cols), BF)],
        scratch=[pltpu.VMEM((rows, cols), BF), pltpu.SemaphoreType.DMA((steps,))],
        out_specs=[AN],
    )(live, front_top, merged1, bulk1_other, land1, inv_top, pivots2)
    return out


def solution(mesh):
    row = P(("sub", "inner"), None)
    placed = (
        row, row, row, P("sub", None), P("sub", None), P("sub", None),
        P(None, ("sub", "inner")), P(("sub", "inner")), P(("sub", "inner")),
    )

    return jax.shard_map(per_device, mesh=mesh, in_specs=placed, out_specs=row, check_vma=False)
```

```python
import jax
import jax.numpy as jnp
from jax import lax
from jax.experimental import pallas as pl
from jax.experimental.pallas import tpu as pltpu
from jax.sharding import PartitionSpec as P


BF = jnp.bfloat16
F32 = jnp.float32
I32 = jnp.int32
NT = (((1,), (1,)), ((), ()))
NN = (((1,), (0,)), ((), ()))
VM = pl.BlockSpec(memory_space=pltpu.VMEM)
VP = pl.BlockSpec(memory_space=pltpu.VMEM)
AN = pl.BlockSpec(memory_space=pltpu.HBM)


def dot(a, b, dims):
    return lax.dot_general(a, b, dims, preferred_element_type=F32)


def swap(value, axis, mask):
    return lax.ppermute(value, axis, [(i, i ^ mask) for i in range(lax.axis_size(axis))])


def later(value, *others):
    return lax.optimization_barrier((value,) + others)[0]


def call(body, in_specs, outs, scratch=(), out_specs=None):
    made = pl.pallas_call(
        body, in_specs=in_specs, out_specs=out_specs or [VM] * len(outs),
        out_shape=[jax.ShapeDtypeStruct(s, d) for s, d in outs], scratch_shapes=scratch,
        compiler_params=pltpu.CompilerParams(vmem_limit_bytes=16 * 1024 * 1024),
    )

    def run(*args):
        return made(*[
            pltpu.with_memory_space_constraint(a, pltpu.HBM) if spec is AN
            else pltpu.with_memory_space_constraint(a, pltpu.VMEM) if spec is VP else a
            for a, spec in zip(args, in_specs)
        ])

    return run


def copies(sems, pairs):
    made = [pltpu.make_async_copy(a, b, sems.at[i]) for i, (a, b) in enumerate(pairs)]
    for c in made:
        c.start()
    return made


def one_hot(row, count):
    ids = lax.broadcasted_iota(I32, (count, row.shape[1]), 0)
    return jnp.where(ids == row, 1.0, 0.0).astype(BF)


def slots_of(code, rows):
    outward = code >= rows
    flags = jnp.broadcast_to(jnp.where(outward, 1.0, 0.0).astype(BF), (8, rows))
    a = lax.broadcasted_iota(I32, (rows, rows), 0)
    b = lax.broadcasted_iota(I32, (rows, rows), 1)
    upper = jnp.where(a < b, 1.0, 0.0).astype(BF)
    rank = dot(flags, upper, NN)[:1].astype(I32)
    return jnp.where(outward, rank, -1)


def landing_of(code, rows):
    pick = one_hot(slots_of(code, rows), rows // 2)
    target = one_hot(code - rows, rows)
    return dot(target, pick, NT).astype(BF)


def row_picks(code, live, n):
    rows = code.shape[1]
    alive = lax.broadcasted_iota(I32, (1, rows), 1) < live
    shown = jnp.where(alive, code, -1)
    slot = jnp.where(alive, slots_of(code, rows), -1)
    ids = lax.broadcasted_iota(I32, (2 * n, rows), 0)
    pivot = jnp.where(jnp.where(ids < n, ids, ids + (rows - n)) == shown, 1.0, 0.0).astype(BF)
    bulk = one_hot(slot, rows // 2)
    return jnp.concatenate([pivot, bulk], 0)


def own_pick(code, live):
    rows = code.shape[1]
    return one_hot(jnp.where(lax.broadcasted_iota(I32, (1, rows), 1) < live, code, -1), rows)


def scaled(panel, inverse):
    block = inverse.shape[1]
    parts = [
        dot(panel[:, b * block:(b + 1) * block], inverse[b * block:(b + 1) * block], NT)
        for b in range(inverse.shape[0] // block)
    ]
    return jnp.concatenate(parts, 1)


def factor_of(panel, inverse, live):
    mask = lax.broadcasted_iota(I32, (panel.shape[0], 1), 0) < live
    return jnp.where(mask, scaled(panel, inverse), 0.0).astype(BF)


def reordered(value, outer, middle):
    rows = value.shape[0]
    part = rows // (outer * middle)
    if middle == 1:
        return value
    if part % 16 == 0:
        return jnp.concatenate(
            [value[(o * middle + m) * part:(o * middle + m + 1) * part]
             for m in range(middle) for o in range(outer)], 0)
    target = lax.broadcasted_iota(I32, (rows, rows), 0)
    source = lax.broadcasted_iota(I32, (rows, rows), 1)
    k = target % part
    o = target // part % outer
    m = target // (part * outer)
    return dot(jnp.where((o * middle + m) * part + k == source, 1.0, 0.0).astype(BF), value, NN).astype(BF)


def spread(block):
    if lax.axis_size("inner") != 8 or block.shape[0] % 32:
        return {}
    return {m: swap(block, "inner", m) for m in GATHER_ORDER}


def collect(block, got):
    if not got:
        return [lax.all_gather(block, "inner", axis=0, tiled=True)]
    got = dict(got)
    got[0] = block
    for m in (0,) + GATHER_ORDER:
        got[m + 1] = swap(got[m], "inner", 1)
    return [got[m] for m in range(8)]


GATHER_ORDER = (6, 4, 2)


def pivots_from(blocks, inverse, pivots, middle, inner):
    if len(blocks) == 1:
        pivots[...] = reordered(scaled(blocks[0], inverse).astype(BF), inner, middle)
        return
    size = blocks[0].shape[0]
    part = size // middle
    made = scaled(jnp.concatenate(blocks, 0), inverse).astype(BF)
    for m in range(len(blocks)):
        at = (lax.axis_index("inner") ^ m) * part
        for q in range(middle):
            pivots[pl.ds(pl.multiple_of(q * part * inner + at, part), part), :] = (
                made[m * size + q * part:m * size + (q + 1) * part])


def up16(count):
    return (count + 15) // 16 * 16


def code_row(ref):
    return jnp.concatenate([ref[i:i + 1] for i in range(ref.shape[0])], 1)


def up16(count):
    return (count + 15) // 16 * 16


def per_device(front_leaf, front_mid, front_top, dinv_leaf, dinv_mid, dinv_top, live_rows, map_leaf, map_mid):
    rows = front_leaf.shape[0]
    panel, block = dinv_leaf.shape
    cols = front_leaf.shape[1] - panel
    inner = lax.axis_size("inner")
    half = rows // 2
    n = [cols // (inner << l) for l in range(3)]

    lanes = 128 if rows % 128 == 0 else rows
    code0 = map_leaf.reshape(rows // lanes, lanes)
    code1 = map_mid.reshape(rows // lanes, lanes)
    live = live_rows.reshape(1, 3)

    mr = dinv_mid.shape[0] // 2
    share = dinv_top.shape[0] // inner
    shared = inner == 8 and share % 16 == 0 and lanes == 128 and rows // lanes <= share and 2 * block == panel

    def pack(code0_ref, code1_ref, mid, fmid, ftop, leaf, near, c0v, c1v, head, top_head, sems):
        made = copies(sems, [
            (code0_ref, c0v), (code1_ref, c1v), (leaf.at[:n[0], :panel], head),
            (mid.at[:mr], near.at[:mr, :block]), (mid.at[mr:], near.at[:mr, block:]),
            (fmid.at[:n[1], :panel], near.at[mr + 16:mr + 16 + n[1]]), (ftop.at[:n[2], :panel], top_head),
        ])
        made[0].wait()
        code = code_row(c0v)
        parts = jnp.concatenate([code >> 8, code & 255, jnp.zeros((6, rows), I32)], 0).astype(F32).astype(BF)
        padded = jnp.concatenate([parts, jnp.zeros((8, 2 * panel - rows), BF)], 1)
        near[mr:mr + 16] = jnp.concatenate([padded[:, :panel], padded[:, panel:]], 0)
        for c in made[1:]:
            c.wait()

    near, code0, code1, block0, top_head = call(
        pack, [AN] * 6,
        [((mr + 16 + up16(n[1]), panel), BF), (code0.shape, I32), (code1.shape, I32), ((n[0], panel), BF),
         ((n[2], panel), BF)],
        scratch=[pltpu.SemaphoreType.DMA((7,))],
    )(code0, code1, dinv_mid, front_mid, front_top, front_leaf)
    got0 = spread(block0)
    near_1 = swap(near, "sub", 1)

    def sent(level):
        return [((2 * n[level] + half, cols), BF)] * 2

    def before0(live_ref, code, front, inverse, fs, cs, factor):
        pick = row_picks(code_row(code), live_ref[0:1, 0:0 + 1], n[1])
        factor[...] = factor_of(front[:, :panel], inverse[...], live_ref[0:1, 0:0 + 1])
        cs[...] = dot(pick, front[:, panel:], NN).astype(BF)
        fs[...] = dot(pick, factor[...], NN).astype(BF)

    fs0, cs0, factor0 = call(
        before0, [VM, VM, VP, VP], sent(1) + [((rows, panel), BF)],
    )(live, code0, front_leaf, dinv_leaf)
    blocks0 = collect(block0, got0)

    def chain(middle, count, headed, extra):
        def body(fs, cs, inverse, *refs):
            refs = list(refs)
            head = refs.pop(0) if headed else None
            code_ref, top = (refs.pop(0), refs.pop(0)) if extra else (None, None)
            blocks, (pivots, out, bulk) = refs[:-3], refs[-3:]
            pivots_from([ref[...] for ref in blocks], inverse[...], pivots, middle, inner)
            update = (cs[...].astype(F32) - dot(fs[...], pivots[...], NT)).astype(BF)
            out[:count] = (update[:count].astype(F32) + head[...].astype(F32)).astype(BF) if headed else update[:count]
            out[count:2 * count] = update[count:2 * count]
            if extra:
                tail = slice(2 * count, 2 * count + share)
                at = pl.multiple_of(lax.axis_index("inner") * share, share)
                out[tail, :block] = top[pl.ds(at, share), :]
                code = jnp.concatenate([code_ref[...], jnp.zeros((share - rows // lanes, lanes), I32)], 0)
                out[tail, block:block + lanes] = (code >> 8).astype(F32).astype(BF)
                out[tail, block + lanes:] = (code & 255).astype(F32).astype(BF)
            bulk[...] = update[2 * count:]

        return body

    def after(level, fs, cs, inverse, blocks, head=(), extra=()):
        count = n[level + 1]
        return call(
            chain(1 << level, count, bool(head), bool(extra)),
            [VM] * (3 + len(head) + len(extra) + len(blocks)),
            [((cols, panel), BF), ((2 * count + (share if extra else 0), cols), BF), ((half, cols), BF)],
        )(fs, cs, inverse, *head, *extra, *blocks)

    def own(level, code, factor, front, pivots, parent):
        def body(live_ref, code_ref, factor_ref, front_ref, pivots_ref, parent_ref, out):
            update = (front_ref[:, panel:].astype(F32) - dot(factor_ref[...], pivots_ref[...], NT)).astype(BF)
            pick = own_pick(code_row(code_ref), live_ref[0:1, level:level + 1])
            out[...] = parent_ref[:, :cols].astype(F32) + dot(pick, update, NN)

        return call(body, [VM, VM, VM, VP, VM, VP], [((rows, cols), F32)])(
            live, code, factor, front, pivots, parent)[0]

    pivots0, pivot0, bulk0 = after(0, fs0, cs0, dinv_leaf, blocks0)
    pivot0_other = swap(pivot0, "sub", 1)
    bulk0_other = swap(bulk0, "sub", 1)

    def unpack1(mine, near_ref, inv_mid, heads1, land0):
        sub = lax.axis_index("sub")
        for q, src in enumerate((mine, near_ref)):
            at = ((sub & 1) ^ q) * 2 * mr
            inv_mid[pl.ds(pl.multiple_of(at, mr), mr), :] = src[:mr, :block]
            inv_mid[pl.ds(pl.multiple_of(at + mr, mr), mr), :] = src[:mr, block:]
            heads1[q] = src[mr + 16:]
        packed = near_ref[mr:mr + 16].astype(F32).astype(I32)
        high = jnp.concatenate([packed[0:1], packed[8:9]], 1)[:, :rows]
        low = jnp.concatenate([packed[1:2], packed[9:10]], 1)[:, :rows]
        land0[...] = landing_of(high * 256 + low, rows)

    inv_mid, heads1, land0 = call(
        unpack1, [VM] * 2,
        [(dinv_leaf.shape, BF), ((2, up16(n[1]), panel), BF), ((rows, half), BF)],
    )(near, later(near_1, pivot0))

    def early1(live_ref, code, front, pick_out, cs):
        pick = row_picks(code_row(code), live_ref[0:1, 1:1 + 1], n[2])
        pick_out[...] = pick
        cs[...] = dot(pick, front[:, panel:], NN).astype(BF)

    pick1, cs1 = call(
        early1, [VM, VM, VP], [((2 * n[2] + half, rows), BF)] + sent(2)[:1],
    )(live, later(code1, pivot0), front_mid)

    def raised(count, flip, headed, extra):
        def body(*refs):
            heads, others, out = refs[0] if headed else None, refs[headed:-1], refs[-1]
            sub = lax.axis_index("sub")

            def ordered(made):
                bit = 1
                while len(made) > 1:
                    low = (sub & bit) == 0
                    made = [
                        jnp.concatenate([jnp.where(low, a, b), jnp.where(low, b, a)], 0)
                        for a, b in zip(made[::2], made[1::2])
                    ]
                    bit *= 2
                return made[0]

            made = [
                others[q][:count].astype(F32) + others[q ^ flip][count:2 * count].astype(F32)
                for q in range(len(others))
            ]
            if headed:
                made = [heads[q][:count].astype(F32) + part for q, part in enumerate(made)]
            total = ordered(made)
            size = total.shape[0]
            out[:size] = total.astype(BF)
            if extra:
                tops = ordered([ref[2 * count:2 * count + share, :block].astype(F32) for ref in others]).astype(BF)
                for q in range(len(others)):
                    at = size + q // 2 * share
                    lane = q % 2 * block
                    out[at:at + share, lane:lane + block] = tops[q * share:(q + 1) * share]

        return body

    raw1, = call(raised(n[1], 1, 1, False), [VM] * 3, [((2 * n[1], panel), BF)])(
        later(heads1, pick1), pivot0, pivot0_other)
    spread1 = spread(raw1)
    merged0 = own(0, code0, factor0, front_leaf, pivots0, front_mid)

    def before1(live_ref, pick, merged, got, land, inverse, fs, factor):
        assembled = (merged[...] + dot(land[...], got[...], NN)).astype(BF)
        factor[...] = factor_of(assembled, inverse[...], live_ref[0:1, 1:1 + 1])
        fs[...] = dot(pick[...], factor[...], NN).astype(BF)

    fs1, factor1 = call(
        before1, [VM] * 6, sent(2)[:1] + [((rows, panel), BF)],
    )(live, pick1, merged0, bulk0_other, land0, inv_mid)
    blocks1 = collect(raw1, spread1)
    pivots1, pivot1, bulk1 = after(
        1, fs1, cs1, inv_mid, blocks1, (top_head,), (code1, dinv_top) if shared else ())
    others = [pivot1] + [swap(pivot1, "sub", m) for m in (1, 2, 3)]
    bulk1_other = swap(bulk1, "sub", 2)
    raw2, = call(raised(n[2], 2, 0, shared), [VM] * 4, [((4 * n[2] + (2 * share if shared else 0), panel), BF)])(*others)
    spread2 = spread(raw2)
    merged1 = own(1, code1, factor1, front_mid, pivots1, front_top)
    blocks2 = collect(raw2, spread2)

    def landing1(src, land1):
        if not shared:
            land1[...] = landing_of(code_row(src), rows)
            return
        packed = src[2 * n[2]:, block:].astype(F32).astype(I32)
        code = packed[:rows // lanes, :lanes] * 256 + packed[:rows // lanes, lanes:]
        land1[...] = landing_of(jnp.concatenate([code[i:i + 1] for i in range(rows // lanes)], 1), rows)

    far1 = others[2] if shared else swap(code1, "sub", 2)
    land1, = call(landing1, [VM], [((rows, half), BF)])(later(far1, raw2))

    if shared:
        def last_pivots(*refs):
            blocks, pivots, inv_top = refs[:-2], refs[-2], refs[-1]
            size = 4 * n[2]
            for m, ref in enumerate(blocks):
                for q in range(4):
                    at = q * inner * share + (lax.axis_index("inner") ^ m) * share
                    row, lane = size + q // 2 * share, q % 2 * block
                    inv_top[pl.ds(pl.multiple_of(at, share), share), :] = ref[row:row + share, lane:lane + block]
            pivots_from([ref[:size] for ref in blocks], inv_top[...], pivots, 4, inner)

        pivots2, inv_top = call(
            last_pivots, [VM] * len(blocks2), [((cols, panel), BF), (dinv_leaf.shape, BF)])(*blocks2)
    else:
        def last_pivots(inverse, *refs):
            pivots_from([ref[...] for ref in refs[:-1]], inverse[...], refs[-1], 4, inner)

        sub = lax.axis_index("sub")
        inv_top = dinv_top
        for bit in (1, 2):
            other = swap(inv_top, "sub", bit)
            inv_top = jnp.where(
                sub & bit == 0, jnp.concatenate([inv_top, other], 0), jnp.concatenate([other, inv_top], 0))
        pivots2, = call(last_pivots, [VM] * (1 + len(blocks2)), [((cols, panel), BF)])(inv_top, *blocks2)

    steps = 2 if rows % 32 == 0 else 1
    part = rows // steps

    def level2(live_ref, front, merged, got, land, inverse, pivots, out, ov, sems):
        assembled = (merged[...] + dot(land[...], got[...], NN)).astype(BF)
        factor = factor_of(assembled, inverse[...], live_ref[0:1, 2:2 + 1])
        mask = lax.broadcasted_iota(I32, (rows, 1), 0) < live_ref[0:1, 2:2 + 1]
        writes = []
        for i in range(steps):
            at = slice(i * part, (i + 1) * part)
            product = dot(factor[at], pivots[...], NT)
            ov[at] = jnp.where(mask[at], front[at, panel:].astype(F32) - product, 0.0).astype(BF)
            writes += copies(sems.at[i:i + 1], [(ov.at[at], out.at[at])])
        for write in writes:
            write.wait()

    out, = call(
        level2, [VM, VP] + [VM] * 5, [((rows, cols), BF)],
        scratch=[pltpu.VMEM((rows, cols), BF), pltpu.SemaphoreType.DMA((steps,))],
        out_specs=[AN],
    )(live, front_top, merged1, bulk1_other, land1, inv_top, pivots2)
    return out


def solution(mesh):
    row = P(("sub", "inner"), None)
    placed = (
        row, row, row, P("sub", None), P("sub", None), P("sub", None),
        P(None, ("sub", "inner")), P(("sub", "inner")), P(("sub", "inner")),
    )

    return jax.shard_map(per_device, mesh=mesh, in_specs=placed, out_specs=row, check_vma=False)
```

```python
import jax
import jax.numpy as jnp
from jax import lax
from jax.experimental import pallas as pl
from jax.experimental.pallas import tpu as pltpu
from jax.sharding import PartitionSpec as P


BF = jnp.bfloat16
F32 = jnp.float32
I32 = jnp.int32
NT = (((1,), (1,)), ((), ()))
NN = (((1,), (0,)), ((), ()))
VM = pl.BlockSpec(memory_space=pltpu.VMEM)
VP = pl.BlockSpec(memory_space=pltpu.VMEM)
AN = pl.BlockSpec(memory_space=pltpu.HBM)


def dot(a, b, dims):
    return lax.dot_general(a, b, dims, preferred_element_type=F32)


def swap(value, axis, mask):
    return lax.ppermute(value, axis, [(i, i ^ mask) for i in range(lax.axis_size(axis))])


def later(value, *others):
    return lax.optimization_barrier((value,) + others)[0]


def call(body, in_specs, outs, scratch=(), out_specs=None):
    made = pl.pallas_call(
        body, in_specs=in_specs, out_specs=out_specs or [VM] * len(outs),
        out_shape=[jax.ShapeDtypeStruct(s, d) for s, d in outs], scratch_shapes=scratch,
        compiler_params=pltpu.CompilerParams(vmem_limit_bytes=16 * 1024 * 1024),
    )

    def run(*args):
        return made(*[
            pltpu.with_memory_space_constraint(a, pltpu.HBM) if spec is AN
            else pltpu.with_memory_space_constraint(a, pltpu.VMEM) if spec is VP else a
            for a, spec in zip(args, in_specs)
        ])

    return run


def copies(sems, pairs):
    made = [pltpu.make_async_copy(a, b, sems.at[i]) for i, (a, b) in enumerate(pairs)]
    for c in made:
        c.start()
    return made


def one_hot(row, count):
    ids = lax.broadcasted_iota(I32, (count, row.shape[1]), 0)
    return jnp.where(ids == row, 1.0, 0.0).astype(BF)


def slots_of(code, rows):
    outward = code >= rows
    flags = jnp.broadcast_to(jnp.where(outward, 1.0, 0.0).astype(BF), (8, rows))
    a = lax.broadcasted_iota(I32, (rows, rows), 0)
    b = lax.broadcasted_iota(I32, (rows, rows), 1)
    upper = jnp.where(a < b, 1.0, 0.0).astype(BF)
    rank = dot(flags, upper, NN)[:1].astype(I32)
    return jnp.where(outward, rank, -1)


def landing_of(code, rows):
    pick = one_hot(slots_of(code, rows), rows // 2)
    target = one_hot(code - rows, rows)
    return dot(target, pick, NT).astype(BF)


def row_picks(code, live, n):
    rows = code.shape[1]
    alive = lax.broadcasted_iota(I32, (1, rows), 1) < live
    shown = jnp.where(alive, code, -1)
    slot = jnp.where(alive, slots_of(code, rows), -1)
    ids = lax.broadcasted_iota(I32, (2 * n, rows), 0)
    pivot = jnp.where(jnp.where(ids < n, ids, ids + (rows - n)) == shown, 1.0, 0.0).astype(BF)
    bulk = one_hot(slot, rows // 2)
    return jnp.concatenate([pivot, bulk], 0)


def own_pick(code, live):
    rows = code.shape[1]
    return one_hot(jnp.where(lax.broadcasted_iota(I32, (1, rows), 1) < live, code, -1), rows)


def scaled(panel, inverse):
    block = inverse.shape[1]
    parts = [
        dot(panel[:, b * block:(b + 1) * block], inverse[b * block:(b + 1) * block], NT)
        for b in range(inverse.shape[0] // block)
    ]
    return jnp.concatenate(parts, 1)


def factor_of(panel, inverse, live):
    mask = lax.broadcasted_iota(I32, (panel.shape[0], 1), 0) < live
    return jnp.where(mask, scaled(panel, inverse), 0.0).astype(BF)


def reordered(value, outer, middle):
    rows = value.shape[0]
    part = rows // (outer * middle)
    if middle == 1:
        return value
    if part % 16 == 0:
        return jnp.concatenate(
            [value[(o * middle + m) * part:(o * middle + m + 1) * part]
             for m in range(middle) for o in range(outer)], 0)
    target = lax.broadcasted_iota(I32, (rows, rows), 0)
    source = lax.broadcasted_iota(I32, (rows, rows), 1)
    k = target % part
    o = target // part % outer
    m = target // (part * outer)
    return dot(jnp.where((o * middle + m) * part + k == source, 1.0, 0.0).astype(BF), value, NN).astype(BF)


def spread(block):
    if lax.axis_size("inner") != 8 or block.shape[0] % 32:
        return {}
    return {m: swap(block, "inner", m) for m in GATHER_ORDER}


def collect(block, got):
    if not got:
        return [lax.all_gather(block, "inner", axis=0, tiled=True)]
    got = dict(got)
    got[0] = block
    for m in (0,) + GATHER_ORDER:
        got[m + 1] = swap(got[m], "inner", 1)
    return [got[m] for m in range(8)]


GATHER_ORDER = (6, 4, 2)


def pivots_from(blocks, inverse, pivots, middle, inner):
    if len(blocks) == 1:
        pivots[...] = reordered(scaled(blocks[0], inverse).astype(BF), inner, middle)
        return
    size = blocks[0].shape[0]
    part = size // middle
    made = scaled(jnp.concatenate(blocks, 0), inverse).astype(BF)
    for m in range(len(blocks)):
        at = (lax.axis_index("inner") ^ m) * part
        for q in range(middle):
            pivots[pl.ds(pl.multiple_of(q * part * inner + at, part), part), :] = (
                made[m * size + q * part:m * size + (q + 1) * part])


def up16(count):
    return (count + 15) // 16 * 16


def code_row(ref):
    return jnp.concatenate([ref[i:i + 1] for i in range(ref.shape[0])], 1)


def up16(count):
    return (count + 15) // 16 * 16


def per_device(front_leaf, front_mid, front_top, dinv_leaf, dinv_mid, dinv_top, live_rows, map_leaf, map_mid):
    rows = front_leaf.shape[0]
    panel, block = dinv_leaf.shape
    cols = front_leaf.shape[1] - panel
    inner = lax.axis_size("inner")
    half = rows // 2
    n = [cols // (inner << l) for l in range(3)]

    lanes = 128 if rows % 128 == 0 else rows
    code0 = map_leaf.reshape(rows // lanes, lanes)
    code1 = map_mid.reshape(rows // lanes, lanes)
    live = live_rows.reshape(1, 3)

    mr = dinv_mid.shape[0] // 2
    share = dinv_top.shape[0] // inner
    shared = inner == 8 and share % 16 == 0 and lanes == 128 and rows // lanes <= share and 2 * block == panel

    def pack(code0_ref, code1_ref, mid, fmid, ftop, leaf, near, c0v, c1v, head, top_head, sems):
        made = copies(sems, [
            (code0_ref, c0v), (code1_ref, c1v), (leaf.at[:n[0], :panel], head),
            (mid.at[:mr], near.at[:mr, :block]), (mid.at[mr:], near.at[:mr, block:]),
            (fmid.at[:n[1], :panel], near.at[mr + 16:mr + 16 + n[1]]), (ftop.at[:n[2], :panel], top_head),
        ])
        made[0].wait()
        code = code_row(c0v)
        parts = jnp.concatenate([code >> 8, code & 255, jnp.zeros((6, rows), I32)], 0).astype(F32).astype(BF)
        padded = jnp.concatenate([parts, jnp.zeros((8, 2 * panel - rows), BF)], 1)
        near[mr:mr + 16] = jnp.concatenate([padded[:, :panel], padded[:, panel:]], 0)
        for c in made[1:]:
            c.wait()

    near, code0, code1, block0, top_head = call(
        pack, [AN] * 6,
        [((mr + 16 + up16(n[1]), panel), BF), (code0.shape, I32), (code1.shape, I32), ((n[0], panel), BF),
         ((n[2], panel), BF)],
        scratch=[pltpu.SemaphoreType.DMA((7,))],
    )(code0, code1, dinv_mid, front_mid, front_top, front_leaf)
    got0 = spread(block0)
    near_1 = swap(near, "sub", 1)

    def sent(level):
        return [((2 * n[level] + half, cols), BF)] * 2

    def before0(live_ref, code, front, inverse, fs, cs, factor):
        pick = row_picks(code_row(code), live_ref[0:1, 0:0 + 1], n[1])
        factor[...] = factor_of(front[:, :panel], inverse[...], live_ref[0:1, 0:0 + 1])
        cs[...] = dot(pick, front[:, panel:], NN).astype(BF)
        fs[...] = dot(pick, factor[...], NN).astype(BF)

    fs0, cs0, factor0 = call(
        before0, [VM, VM, VP, VP], sent(1) + [((rows, panel), BF)],
    )(live, code0, front_leaf, dinv_leaf)
    blocks0 = collect(block0, got0)

    def chain(middle, count, headed, extra, parts):
        def body(fs, cs, inverse, *refs):
            refs = list(refs)
            head = refs.pop(0) if headed else None
            code_ref, top = (refs.pop(0), refs.pop(0)) if extra else (None, None)
            bulks = refs[-parts:]
            blocks, (pivots, out) = refs[:-2 - parts], refs[-2 - parts:-parts]
            pivots_from([ref[...] for ref in blocks], inverse[...], pivots, middle, inner)
            update = (cs[...].astype(F32) - dot(fs[...], pivots[...], NT)).astype(BF)
            out[:count] = (update[:count].astype(F32) + head[...].astype(F32)).astype(BF) if headed else update[:count]
            out[count:2 * count] = update[count:2 * count]
            if extra:
                tail = slice(2 * count, 2 * count + share)
                at = pl.multiple_of(lax.axis_index("inner") * share, share)
                out[tail, :block] = top[pl.ds(at, share), :]
                code = jnp.concatenate([code_ref[...], jnp.zeros((share - rows // lanes, lanes), I32)], 0)
                out[tail, block:block + lanes] = (code >> 8).astype(F32).astype(BF)
                out[tail, block + lanes:] = (code & 255).astype(F32).astype(BF)
            for i, bulk in enumerate(bulks):
                bulk[...] = update[2 * count:, i * (cols // parts):(i + 1) * (cols // parts)]

        return body

    def after(level, fs, cs, inverse, blocks, parts, head=(), extra=()):
        count = n[level + 1]
        return call(
            chain(1 << level, count, bool(head), bool(extra), parts),
            [VM] * (3 + len(head) + len(extra) + len(blocks)),
            [((cols, panel), BF), ((2 * count + (share if extra else 0), cols), BF)] + [((half, cols // parts), BF)] * parts,
        )(fs, cs, inverse, *head, *extra, *blocks)

    def own(level, code, factor, front, pivots, parent):
        def body(live_ref, code_ref, factor_ref, front_ref, pivots_ref, parent_ref, out):
            update = (front_ref[:, panel:].astype(F32) - dot(factor_ref[...], pivots_ref[...], NT)).astype(BF)
            pick = own_pick(code_row(code_ref), live_ref[0:1, level:level + 1])
            out[...] = parent_ref[:, :cols].astype(F32) + dot(pick, update, NN)

        return call(body, [VM, VM, VM, VP, VM, VP], [((rows, cols), F32)])(
            live, code, factor, front, pivots, parent)[0]

    pivots0, pivot0, bulk0 = after(0, fs0, cs0, dinv_leaf, blocks0, 1)
    pivot0_other = swap(pivot0, "sub", 1)
    bulk0_other = swap(bulk0, "sub", 1)

    def unpack1(mine, near_ref, inv_mid, heads1, land0):
        sub = lax.axis_index("sub")
        for q, src in enumerate((mine, near_ref)):
            at = ((sub & 1) ^ q) * 2 * mr
            inv_mid[pl.ds(pl.multiple_of(at, mr), mr), :] = src[:mr, :block]
            inv_mid[pl.ds(pl.multiple_of(at + mr, mr), mr), :] = src[:mr, block:]
            heads1[q] = src[mr + 16:]
        packed = near_ref[mr:mr + 16].astype(F32).astype(I32)
        high = jnp.concatenate([packed[0:1], packed[8:9]], 1)[:, :rows]
        low = jnp.concatenate([packed[1:2], packed[9:10]], 1)[:, :rows]
        land0[...] = landing_of(high * 256 + low, rows)

    inv_mid, heads1, land0 = call(
        unpack1, [VM] * 2,
        [(dinv_leaf.shape, BF), ((2, up16(n[1]), panel), BF), ((rows, half), BF)],
    )(near, later(near_1, pivot0))

    def early1(live_ref, code, front, pick_out, cs):
        pick = row_picks(code_row(code), live_ref[0:1, 1:1 + 1], n[2])
        pick_out[...] = pick
        cs[...] = dot(pick, front[:, panel:], NN).astype(BF)

    pick1, cs1 = call(
        early1, [VM, VM, VP], [((2 * n[2] + half, rows), BF)] + sent(2)[:1],
    )(live, later(code1, pivot0), front_mid)

    def raised(count, flip, headed, extra):
        def body(*refs):
            heads, others, out = refs[0] if headed else None, refs[headed:-1], refs[-1]
            sub = lax.axis_index("sub")

            def ordered(made):
                bit = 1
                while len(made) > 1:
                    low = (sub & bit) == 0
                    made = [
                        jnp.concatenate([jnp.where(low, a, b), jnp.where(low, b, a)], 0)
                        for a, b in zip(made[::2], made[1::2])
                    ]
                    bit *= 2
                return made[0]

            made = [
                others[q][:count].astype(F32) + others[q ^ flip][count:2 * count].astype(F32)
                for q in range(len(others))
            ]
            if headed:
                made = [heads[q][:count].astype(F32) + part for q, part in enumerate(made)]
            total = ordered(made)
            size = total.shape[0]
            out[:size] = total.astype(BF)
            if extra:
                tops = ordered([ref[2 * count:2 * count + share, :block].astype(F32) for ref in others]).astype(BF)
                for q in range(len(others)):
                    at = size + q // 2 * share
                    lane = q % 2 * block
                    out[at:at + share, lane:lane + block] = tops[q * share:(q + 1) * share]

        return body

    raw1, = call(raised(n[1], 1, 1, False), [VM] * 3, [((2 * n[1], panel), BF)])(
        later(heads1, pick1), pivot0, pivot0_other)
    spread1 = spread(raw1)
    merged0 = own(0, code0, factor0, front_leaf, pivots0, front_mid)

    def before1(live_ref, pick, merged, got, land, inverse, fs, factor):
        assembled = (merged[...] + dot(land[...], got[...], NN)).astype(BF)
        factor[...] = factor_of(assembled, inverse[...], live_ref[0:1, 1:1 + 1])
        fs[...] = dot(pick[...], factor[...], NN).astype(BF)

    fs1, factor1 = call(
        before1, [VM] * 6, sent(2)[:1] + [((rows, panel), BF)],
    )(live, pick1, merged0, bulk0_other, land0, inv_mid)
    blocks1 = collect(raw1, spread1)
    pivots1, pivot1, *bulk1 = after(
        1, fs1, cs1, inv_mid, blocks1, panel // block, (top_head,), (code1, dinv_top) if shared else ())
    others = [pivot1] + [swap(pivot1, "sub", m) for m in (1, 2, 3)]
    bulk1_other = [swap(part, "sub", 2) for part in bulk1]
    raw2, = call(raised(n[2], 2, 0, shared), [VM] * 4, [((4 * n[2] + (2 * share if shared else 0), panel), BF)])(*others)
    spread2 = spread(raw2)
    merged1 = own(1, code1, factor1, front_mid, pivots1, front_top)
    blocks2 = collect(raw2, spread2)

    def landing1(src, land1):
        if not shared:
            land1[...] = landing_of(code_row(src), rows)
            return
        packed = src[2 * n[2]:, block:].astype(F32).astype(I32)
        code = packed[:rows // lanes, :lanes] * 256 + packed[:rows // lanes, lanes:]
        land1[...] = landing_of(jnp.concatenate([code[i:i + 1] for i in range(rows // lanes)], 1), rows)

    far1 = others[2] if shared else swap(code1, "sub", 2)
    land1, = call(landing1, [VM], [((rows, half), BF)])(later(far1, raw2))

    if shared:
        def last_pivots(*refs):
            blocks, pivots, inv_top = refs[:-2], refs[-2], refs[-1]
            size = 4 * n[2]
            for m, ref in enumerate(blocks):
                for q in range(4):
                    at = q * inner * share + (lax.axis_index("inner") ^ m) * share
                    row, lane = size + q // 2 * share, q % 2 * block
                    inv_top[pl.ds(pl.multiple_of(at, share), share), :] = ref[row:row + share, lane:lane + block]
            pivots_from([ref[:size] for ref in blocks], inv_top[...], pivots, 4, inner)

        pivots2, inv_top = call(
            last_pivots, [VM] * len(blocks2), [((cols, panel), BF), (dinv_leaf.shape, BF)])(*blocks2)
    else:
        def last_pivots(inverse, *refs):
            pivots_from([ref[...] for ref in refs[:-1]], inverse[...], refs[-1], 4, inner)

        sub = lax.axis_index("sub")
        inv_top = dinv_top
        for bit in (1, 2):
            other = swap(inv_top, "sub", bit)
            inv_top = jnp.where(
                sub & bit == 0, jnp.concatenate([inv_top, other], 0), jnp.concatenate([other, inv_top], 0))
        pivots2, = call(last_pivots, [VM] * (1 + len(blocks2)), [((cols, panel), BF)])(inv_top, *blocks2)

    def level2_part(i, first, last):
        lane = slice(i * block, (i + 1) * block)

        def body(live_ref, merged, got, land, inverse, pivots, so_far, out, *scratch):
            assembled = (merged[:, lane] + dot(land[...], got[...], NN)).astype(BF)
            factor = factor_of(assembled, inverse[lane], live_ref[0:1, 2:3])
            if not last:
                out[...] = (so_far[:, panel:].astype(F32) if first else so_far[...]) - dot(factor, pivots[:, lane], NT)
                return
            ov, sems = scratch
            mask = lax.broadcasted_iota(I32, (rows, 1), 0) < live_ref[0:1, 2:3]
            writes = []
            for k in range(steps):
                at = slice(k * part, (k + 1) * part)
                start = so_far[at, panel:].astype(F32) if first else so_far[at]
                ov[at] = jnp.where(mask[at], start - dot(factor[at], pivots[:, lane], NT), 0.0).astype(BF)
                writes += copies(sems.at[k:k + 1], [(ov.at[at], out.at[at])])
            for write in writes:
                write.wait()

        return body

    steps = 2 if rows % 32 == 0 else 1
    part = rows // steps
    count = panel // block
    result = front_top
    for i in range(count):
        last = i == count - 1
        result, = call(
            level2_part(i, i == 0, last), [VM] * 6 + [VP if i == 0 else VM],
            [((rows, cols), BF if last else F32)],
            scratch=[pltpu.VMEM((rows, cols), BF), pltpu.SemaphoreType.DMA((steps,))] if last else (),
            out_specs=[AN] if last else None,
        )(live, merged1, bulk1_other[i], land1, inv_top, pivots2, result)
    return result


def solution(mesh):
    row = P(("sub", "inner"), None)
    placed = (
        row, row, row, P("sub", None), P("sub", None), P("sub", None),
        P(None, ("sub", "inner")), P(("sub", "inner")), P(("sub", "inner")),
    )

    return jax.shard_map(per_device, mesh=mesh, in_specs=placed, out_specs=row, check_vma=False)
```

```python
import jax
import jax.numpy as jnp
from jax import lax
from jax.experimental import pallas as pl
from jax.experimental.pallas import tpu as pltpu
from jax.sharding import PartitionSpec as P


BF = jnp.bfloat16
F32 = jnp.float32
I32 = jnp.int32
NT = (((1,), (1,)), ((), ()))
NN = (((1,), (0,)), ((), ()))
VM = pl.BlockSpec(memory_space=pltpu.VMEM)
VP = pl.BlockSpec(memory_space=pltpu.VMEM)
AN = pl.BlockSpec(memory_space=pltpu.HBM)


def dot(a, b, dims):
    return lax.dot_general(a, b, dims, preferred_element_type=F32)


def swap(value, axis, mask):
    return lax.ppermute(value, axis, [(i, i ^ mask) for i in range(lax.axis_size(axis))])


def later(value, *others):
    return lax.optimization_barrier((value,) + others)[0]


def call(body, in_specs, outs, scratch=(), out_specs=None):
    made = pl.pallas_call(
        body, in_specs=in_specs, out_specs=out_specs or [VM] * len(outs),
        out_shape=[jax.ShapeDtypeStruct(s, d) for s, d in outs], scratch_shapes=scratch,
        compiler_params=pltpu.CompilerParams(vmem_limit_bytes=16 * 1024 * 1024),
    )

    def run(*args):
        return made(*[
            pltpu.with_memory_space_constraint(a, pltpu.HBM) if spec is AN
            else pltpu.with_memory_space_constraint(a, pltpu.VMEM) if spec is VP else a
            for a, spec in zip(args, in_specs)
        ])

    return run


def copies(sems, pairs):
    made = [pltpu.make_async_copy(a, b, sems.at[i]) for i, (a, b) in enumerate(pairs)]
    for c in made:
        c.start()
    return made


def one_hot(row, count):
    ids = lax.broadcasted_iota(I32, (count, row.shape[1]), 0)
    return jnp.where(ids == row, 1.0, 0.0).astype(BF)


def slots_of(code, rows):
    outward = code >= rows
    flags = jnp.broadcast_to(jnp.where(outward, 1.0, 0.0).astype(BF), (8, rows))
    a = lax.broadcasted_iota(I32, (rows, rows), 0)
    b = lax.broadcasted_iota(I32, (rows, rows), 1)
    upper = jnp.where(a < b, 1.0, 0.0).astype(BF)
    rank = dot(flags, upper, NN)[:1].astype(I32)
    return jnp.where(outward, rank, -1)


def landing_of(code, rows):
    pick = one_hot(slots_of(code, rows), rows // 2)
    target = one_hot(code - rows, rows)
    return dot(target, pick, NT).astype(BF)


def row_picks(code, live, n):
    rows = code.shape[1]
    alive = lax.broadcasted_iota(I32, (1, rows), 1) < live
    shown = jnp.where(alive, code, -1)
    slot = jnp.where(alive, slots_of(code, rows), -1)
    ids = lax.broadcasted_iota(I32, (2 * n, rows), 0)
    pivot = jnp.where(jnp.where(ids < n, ids, ids + (rows - n)) == shown, 1.0, 0.0).astype(BF)
    bulk = one_hot(slot, rows // 2)
    return jnp.concatenate([pivot, bulk], 0)


def own_pick(code, live):
    rows = code.shape[1]
    return one_hot(jnp.where(lax.broadcasted_iota(I32, (1, rows), 1) < live, code, -1), rows)


def scaled(panel, inverse):
    block = inverse.shape[1]
    parts = [
        dot(panel[:, b * block:(b + 1) * block], inverse[b * block:(b + 1) * block], NT)
        for b in range(inverse.shape[0] // block)
    ]
    return jnp.concatenate(parts, 1)


def factor_of(panel, inverse, live):
    mask = lax.broadcasted_iota(I32, (panel.shape[0], 1), 0) < live
    return jnp.where(mask, scaled(panel, inverse), 0.0).astype(BF)


def reordered(value, outer, middle):
    rows = value.shape[0]
    part = rows // (outer * middle)
    if middle == 1:
        return value
    if part % 16 == 0:
        return jnp.concatenate(
            [value[(o * middle + m) * part:(o * middle + m + 1) * part]
             for m in range(middle) for o in range(outer)], 0)
    target = lax.broadcasted_iota(I32, (rows, rows), 0)
    source = lax.broadcasted_iota(I32, (rows, rows), 1)
    k = target % part
    o = target // part % outer
    m = target // (part * outer)
    return dot(jnp.where((o * middle + m) * part + k == source, 1.0, 0.0).astype(BF), value, NN).astype(BF)


def spread(block):
    if lax.axis_size("inner") != 8 or block.shape[0] % 32:
        return {}
    return {m: swap(block, "inner", m) for m in GATHER_ORDER}


def collect(block, got):
    if not got:
        return [lax.all_gather(block, "inner", axis=0, tiled=True)]
    got = dict(got)
    got[0] = block
    for m in (0,) + GATHER_ORDER:
        got[m + 1] = swap(got[m], "inner", 1)
    return [got[m] for m in range(8)]


GATHER_ORDER = (6, 4, 2)


def pivots_from(blocks, inverse, pivots, middle, inner):
    if len(blocks) == 1:
        pivots[...] = reordered(scaled(blocks[0], inverse).astype(BF), inner, middle)
        return
    size = blocks[0].shape[0]
    part = size // middle
    made = scaled(jnp.concatenate(blocks, 0), inverse).astype(BF)
    for m in range(len(blocks)):
        at = (lax.axis_index("inner") ^ m) * part
        for q in range(middle):
            pivots[pl.ds(pl.multiple_of(q * part * inner + at, part), part), :] = (
                made[m * size + q * part:m * size + (q + 1) * part])


def up16(count):
    return (count + 15) // 16 * 16


def code_row(ref):
    return jnp.concatenate([ref[i:i + 1] for i in range(ref.shape[0])], 1)


def up16(count):
    return (count + 15) // 16 * 16


def per_device(front_leaf, front_mid, front_top, dinv_leaf, dinv_mid, dinv_top, live_rows, map_leaf, map_mid):
    rows = front_leaf.shape[0]
    panel, block = dinv_leaf.shape
    cols = front_leaf.shape[1] - panel
    inner = lax.axis_size("inner")
    half = rows // 2
    n = [cols // (inner << l) for l in range(3)]

    lanes = 128 if rows % 128 == 0 else rows
    code0 = map_leaf.reshape(rows // lanes, lanes)
    code1 = map_mid.reshape(rows // lanes, lanes)
    live = live_rows.reshape(1, 3)

    mr = dinv_mid.shape[0] // 2
    share = dinv_top.shape[0] // inner
    shared = inner == 8 and share % 16 == 0 and lanes == 128 and rows // lanes <= share and 2 * block == panel

    def pack(code0_ref, code1_ref, mid, fmid, ftop, leaf, near, c0v, c1v, head, top_head, sems):
        made = copies(sems, [
            (code0_ref, c0v), (code1_ref, c1v), (leaf.at[:n[0], :panel], head),
            (mid.at[:mr], near.at[:mr, :block]), (mid.at[mr:], near.at[:mr, block:]),
            (fmid.at[:n[1], :panel], near.at[mr + 16:mr + 16 + n[1]]), (ftop.at[:n[2], :panel], top_head),
        ])
        made[0].wait()
        code = code_row(c0v)
        parts = jnp.concatenate([code >> 8, code & 255, jnp.zeros((6, rows), I32)], 0).astype(F32).astype(BF)
        padded = jnp.concatenate([parts, jnp.zeros((8, 2 * panel - rows), BF)], 1)
        near[mr:mr + 16] = jnp.concatenate([padded[:, :panel], padded[:, panel:]], 0)
        for c in made[1:]:
            c.wait()

    near, code0, code1, block0, top_head = call(
        pack, [AN] * 6,
        [((mr + 16 + up16(n[1]), panel), BF), (code0.shape, I32), (code1.shape, I32), ((n[0], panel), BF),
         ((n[2], panel), BF)],
        scratch=[pltpu.SemaphoreType.DMA((7,))],
    )(code0, code1, dinv_mid, front_mid, front_top, front_leaf)
    got0 = spread(block0)
    near_1 = swap(near, "sub", 1)

    def sent(level):
        return [((2 * n[level] + half, cols), BF)] * 2

    def before0(live_ref, code, front, inverse, fs, cs, factor):
        pick = row_picks(code_row(code), live_ref[0:1, 0:0 + 1], n[1])
        factor[...] = factor_of(front[:, :panel], inverse[...], live_ref[0:1, 0:0 + 1])
        cs[...] = dot(pick, front[:, panel:], NN).astype(BF)
        fs[...] = dot(pick, factor[...], NN).astype(BF)

    fs0, cs0, factor0 = call(
        before0, [VM, VM, VP, VP], sent(1) + [((rows, panel), BF)],
    )(live, code0, front_leaf, dinv_leaf)
    blocks0 = collect(block0, got0)

    def chain(middle, count, headed, extra, parts):
        def body(fs, cs, inverse, *refs):
            refs = list(refs)
            head = refs.pop(0) if headed else None
            code_ref, top = (refs.pop(0), refs.pop(0)) if extra else (None, None)
            at = len(refs) - parts
            blocks, (pivots, out), bulks = refs[:at - 2], refs[at - 2:at], refs[at:]
            pivots_from([ref[...] for ref in blocks], inverse[...], pivots, middle, inner)
            used = slice(None) if parts else slice(0, 2 * count)
            update = (cs[used].astype(F32) - dot(fs[used], pivots[...], NT)).astype(BF)
            out[:count] = (update[:count].astype(F32) + head[...].astype(F32)).astype(BF) if headed else update[:count]
            out[count:2 * count] = update[count:2 * count]
            if extra:
                tail = slice(2 * count, 2 * count + share)
                at = pl.multiple_of(lax.axis_index("inner") * share, share)
                out[tail, :block] = top[pl.ds(at, share), :]
                code = jnp.concatenate([code_ref[...], jnp.zeros((share - rows // lanes, lanes), I32)], 0)
                out[tail, block:block + lanes] = (code >> 8).astype(F32).astype(BF)
                out[tail, block + lanes:] = (code & 255).astype(F32).astype(BF)
            for i, bulk in enumerate(bulks):
                bulk[...] = update[2 * count:, i * (cols // parts):(i + 1) * (cols // parts)]

        return body

    def after(level, fs, cs, inverse, blocks, parts, head=(), extra=()):
        count = n[level + 1]
        return call(
            chain(1 << level, count, bool(head), bool(extra), parts),
            [VM] * (3 + len(head) + len(extra) + len(blocks)),
            [((cols, panel), BF), ((2 * count + (share if extra else 0), cols), BF)] + [((half, cols // max(parts, 1)), BF)] * parts,
        )(fs, cs, inverse, *head, *extra, *blocks)

    def own(level, code, factor, front, pivots, parent):
        def body(live_ref, code_ref, factor_ref, front_ref, pivots_ref, parent_ref, out):
            update = (front_ref[:, panel:].astype(F32) - dot(factor_ref[...], pivots_ref[...], NT)).astype(BF)
            pick = own_pick(code_row(code_ref), live_ref[0:1, level:level + 1])
            out[...] = parent_ref[:, :cols].astype(F32) + dot(pick, update, NN)

        return call(body, [VM, VM, VM, VP, VM, VP], [((rows, cols), F32)])(
            live, code, factor, front, pivots, parent)[0]

    def rest(fs, cs, pivots, out):
        out[...] = (cs[2 * n[1]:].astype(F32) - dot(fs[2 * n[1]:], pivots[...], NT)).astype(BF)

    pivots0, pivot0 = after(0, fs0, cs0, dinv_leaf, blocks0, 0)
    bulk0, = call(rest, [VM] * 3, [((half, cols), BF)])(fs0, cs0, pivots0)
    pivot0_other = swap(pivot0, "sub", 1)
    bulk0_other = swap(bulk0, "sub", 1)

    def unpack1(mine, near_ref, inv_mid, heads1, land0):
        sub = lax.axis_index("sub")
        for q, src in enumerate((mine, near_ref)):
            at = ((sub & 1) ^ q) * 2 * mr
            inv_mid[pl.ds(pl.multiple_of(at, mr), mr), :] = src[:mr, :block]
            inv_mid[pl.ds(pl.multiple_of(at + mr, mr), mr), :] = src[:mr, block:]
            heads1[q] = src[mr + 16:]
        packed = near_ref[mr:mr + 16].astype(F32).astype(I32)
        high = jnp.concatenate([packed[0:1], packed[8:9]], 1)[:, :rows]
        low = jnp.concatenate([packed[1:2], packed[9:10]], 1)[:, :rows]
        land0[...] = landing_of(high * 256 + low, rows)

    inv_mid, heads1, land0 = call(
        unpack1, [VM] * 2,
        [(dinv_leaf.shape, BF), ((2, up16(n[1]), panel), BF), ((rows, half), BF)],
    )(near, later(near_1, pivot0))

    def early1(live_ref, code, front, pick_out, cs):
        pick = row_picks(code_row(code), live_ref[0:1, 1:1 + 1], n[2])
        pick_out[...] = pick
        cs[...] = dot(pick, front[:, panel:], NN).astype(BF)

    pick1, cs1 = call(
        early1, [VM, VM, VP], [((2 * n[2] + half, rows), BF)] + sent(2)[:1],
    )(live, later(code1, pivot0), front_mid)

    def raised(count, flip, headed, extra):
        def body(*refs):
            heads, others, out = refs[0] if headed else None, refs[headed:-1], refs[-1]
            sub = lax.axis_index("sub")

            def ordered(made):
                bit = 1
                while len(made) > 1:
                    low = (sub & bit) == 0
                    made = [
                        jnp.concatenate([jnp.where(low, a, b), jnp.where(low, b, a)], 0)
                        for a, b in zip(made[::2], made[1::2])
                    ]
                    bit *= 2
                return made[0]

            made = [
                others[q][:count].astype(F32) + others[q ^ flip][count:2 * count].astype(F32)
                for q in range(len(others))
            ]
            if headed:
                made = [heads[q][:count].astype(F32) + part for q, part in enumerate(made)]
            total = ordered(made)
            size = total.shape[0]
            out[:size] = total.astype(BF)
            if extra:
                tops = ordered([ref[2 * count:2 * count + share, :block].astype(F32) for ref in others]).astype(BF)
                for q in range(len(others)):
                    at = size + q // 2 * share
                    lane = q % 2 * block
                    out[at:at + share, lane:lane + block] = tops[q * share:(q + 1) * share]

        return body

    raw1, = call(raised(n[1], 1, 1, False), [VM] * 3, [((2 * n[1], panel), BF)])(
        later(heads1, pick1), pivot0, pivot0_other)
    spread1 = spread(raw1)
    merged0 = own(0, code0, factor0, front_leaf, pivots0, front_mid)

    def before1(live_ref, pick, merged, got, land, inverse, fs, factor):
        assembled = (merged[...] + dot(land[...], got[...], NN)).astype(BF)
        factor[...] = factor_of(assembled, inverse[...], live_ref[0:1, 1:1 + 1])
        fs[...] = dot(pick[...], factor[...], NN).astype(BF)

    fs1, factor1 = call(
        before1, [VM] * 6, sent(2)[:1] + [((rows, panel), BF)],
    )(live, pick1, merged0, bulk0_other, land0, inv_mid)
    blocks1 = collect(raw1, spread1)
    pivots1, pivot1, *bulk1 = after(
        1, fs1, cs1, inv_mid, blocks1, panel // block, (top_head,), (code1, dinv_top) if shared else ())
    others = [pivot1] + [swap(pivot1, "sub", m) for m in (1, 2, 3)]
    bulk1_other = [swap(part, "sub", 2) for part in bulk1]
    raw2, = call(raised(n[2], 2, 0, shared), [VM] * 4, [((4 * n[2] + (2 * share if shared else 0), panel), BF)])(*others)
    spread2 = spread(raw2)
    merged1 = own(1, code1, factor1, front_mid, pivots1, front_top)
    blocks2 = collect(raw2, spread2)

    def landing1(src, land1):
        if not shared:
            land1[...] = landing_of(code_row(src), rows)
            return
        packed = src[2 * n[2]:, block:].astype(F32).astype(I32)
        code = packed[:rows // lanes, :lanes] * 256 + packed[:rows // lanes, lanes:]
        land1[...] = landing_of(jnp.concatenate([code[i:i + 1] for i in range(rows // lanes)], 1), rows)

    far1 = others[2] if shared else swap(code1, "sub", 2)
    land1, = call(landing1, [VM], [((rows, half), BF)])(later(far1, raw2))

    if shared:
        def last_pivots(*refs):
            blocks, pivots, inv_top = refs[:-2], refs[-2], refs[-1]
            size = 4 * n[2]
            for m, ref in enumerate(blocks):
                for q in range(4):
                    at = q * inner * share + (lax.axis_index("inner") ^ m) * share
                    row, lane = size + q // 2 * share, q % 2 * block
                    inv_top[pl.ds(pl.multiple_of(at, share), share), :] = ref[row:row + share, lane:lane + block]
            pivots_from([ref[:size] for ref in blocks], inv_top[...], pivots, 4, inner)

        pivots2, inv_top = call(
            last_pivots, [VM] * len(blocks2), [((cols, panel), BF), (dinv_leaf.shape, BF)])(*blocks2)
    else:
        def last_pivots(inverse, *refs):
            pivots_from([ref[...] for ref in refs[:-1]], inverse[...], refs[-1], 4, inner)

        sub = lax.axis_index("sub")
        inv_top = dinv_top
        for bit in (1, 2):
            other = swap(inv_top, "sub", bit)
            inv_top = jnp.where(
                sub & bit == 0, jnp.concatenate([inv_top, other], 0), jnp.concatenate([other, inv_top], 0))
        pivots2, = call(last_pivots, [VM] * (1 + len(blocks2)), [((cols, panel), BF)])(inv_top, *blocks2)

    def level2_part(i, first, last):
        lane = slice(i * block, (i + 1) * block)

        def body(live_ref, merged, got, land, inverse, pivots, so_far, out, *scratch):
            assembled = (merged[:, lane] + dot(land[...], got[...], NN)).astype(BF)
            factor = factor_of(assembled, inverse[lane], live_ref[0:1, 2:3])
            if not last:
                out[...] = (so_far[:, panel:].astype(F32) if first else so_far[...]) - dot(factor, pivots[:, lane], NT)
                return
            ov, sems = scratch
            mask = lax.broadcasted_iota(I32, (rows, 1), 0) < live_ref[0:1, 2:3]
            writes = []
            for k in range(steps):
                at = slice(k * part, (k + 1) * part)
                start = so_far[at, panel:].astype(F32) if first else so_far[at]
                ov[at] = jnp.where(mask[at], start - dot(factor[at], pivots[:, lane], NT), 0.0).astype(BF)
                writes += copies(sems.at[k:k + 1], [(ov.at[at], out.at[at])])
            for write in writes:
                write.wait()

        return body

    steps = 2 if rows % 32 == 0 else 1
    part = rows // steps
    count = panel // block
    result = front_top
    for i in range(count):
        last = i == count - 1
        result, = call(
            level2_part(i, i == 0, last), [VM] * 6 + [VP if i == 0 else VM],
            [((rows, cols), BF if last else F32)],
            scratch=[pltpu.VMEM((rows, cols), BF), pltpu.SemaphoreType.DMA((steps,))] if last else (),
            out_specs=[AN] if last else None,
        )(live, merged1, bulk1_other[i], land1, inv_top, pivots2, result)
    return result


def solution(mesh):
    row = P(("sub", "inner"), None)
    placed = (
        row, row, row, P("sub", None), P("sub", None), P("sub", None),
        P(None, ("sub", "inner")), P(("sub", "inner")), P(("sub", "inner")),
    )

    return jax.shard_map(per_device, mesh=mesh, in_specs=placed, out_specs=row, check_vma=False)
```

```python
import jax
import jax.numpy as jnp
from jax import lax
from jax.experimental import pallas as pl
from jax.experimental.pallas import tpu as pltpu
from jax.sharding import PartitionSpec as P


BF = jnp.bfloat16
F32 = jnp.float32
I32 = jnp.int32
NT = (((1,), (1,)), ((), ()))
NN = (((1,), (0,)), ((), ()))
VM = pl.BlockSpec(memory_space=pltpu.VMEM)
VP = pl.BlockSpec(memory_space=pltpu.VMEM)
AN = pl.BlockSpec(memory_space=pltpu.HBM)


def dot(a, b, dims):
    return lax.dot_general(a, b, dims, preferred_element_type=F32)


def swap(value, axis, mask):
    return lax.ppermute(value, axis, [(i, i ^ mask) for i in range(lax.axis_size(axis))])


def later(value, *others):
    return lax.optimization_barrier((value,) + others)[0]


def call(body, in_specs, outs, scratch=(), out_specs=None):
    made = pl.pallas_call(
        body, in_specs=in_specs, out_specs=out_specs or [VM] * len(outs),
        out_shape=[jax.ShapeDtypeStruct(s, d) for s, d in outs], scratch_shapes=scratch,
        compiler_params=pltpu.CompilerParams(vmem_limit_bytes=16 * 1024 * 1024),
    )

    def run(*args):
        return made(*[
            pltpu.with_memory_space_constraint(a, pltpu.HBM) if spec is AN
            else pltpu.with_memory_space_constraint(a, pltpu.VMEM) if spec is VP else a
            for a, spec in zip(args, in_specs)
        ])

    return run


def copies(sems, pairs):
    made = [pltpu.make_async_copy(a, b, sems.at[i]) for i, (a, b) in enumerate(pairs)]
    for c in made:
        c.start()
    return made


def one_hot(row, count):
    ids = lax.broadcasted_iota(I32, (count, row.shape[1]), 0)
    return jnp.where(ids == row, 1.0, 0.0).astype(BF)


def slots_of(code, rows):
    outward = code >= rows
    flags = jnp.broadcast_to(jnp.where(outward, 1.0, 0.0).astype(BF), (8, rows))
    a = lax.broadcasted_iota(I32, (rows, rows), 0)
    b = lax.broadcasted_iota(I32, (rows, rows), 1)
    upper = jnp.where(a < b, 1.0, 0.0).astype(BF)
    rank = dot(flags, upper, NN)[:1].astype(I32)
    return jnp.where(outward, rank, -1)


def landing_of(code, rows):
    pick = one_hot(slots_of(code, rows), rows // 2)
    target = one_hot(code - rows, rows)
    return dot(target, pick, NT).astype(BF)


def row_picks(code, live, n):
    rows = code.shape[1]
    alive = lax.broadcasted_iota(I32, (1, rows), 1) < live
    shown = jnp.where(alive, code, -1)
    slot = jnp.where(alive, slots_of(code, rows), -1)
    ids = lax.broadcasted_iota(I32, (2 * n, rows), 0)
    pivot = jnp.where(jnp.where(ids < n, ids, ids + (rows - n)) == shown, 1.0, 0.0).astype(BF)
    bulk = one_hot(slot, rows // 2)
    return jnp.concatenate([pivot, bulk], 0)


def own_pick(code, live):
    rows = code.shape[1]
    return one_hot(jnp.where(lax.broadcasted_iota(I32, (1, rows), 1) < live, code, -1), rows)


def scaled(panel, inverse):
    block = inverse.shape[1]
    parts = [
        dot(panel[:, b * block:(b + 1) * block], inverse[b * block:(b + 1) * block], NT)
        for b in range(inverse.shape[0] // block)
    ]
    return jnp.concatenate(parts, 1)


def factor_of(panel, inverse, live):
    mask = lax.broadcasted_iota(I32, (panel.shape[0], 1), 0) < live
    return jnp.where(mask, scaled(panel, inverse), 0.0).astype(BF)


def reordered(value, outer, middle):
    rows = value.shape[0]
    part = rows // (outer * middle)
    if middle == 1:
        return value
    if part % 16 == 0:
        return jnp.concatenate(
            [value[(o * middle + m) * part:(o * middle + m + 1) * part]
             for m in range(middle) for o in range(outer)], 0)
    target = lax.broadcasted_iota(I32, (rows, rows), 0)
    source = lax.broadcasted_iota(I32, (rows, rows), 1)
    k = target % part
    o = target // part % outer
    m = target // (part * outer)
    return dot(jnp.where((o * middle + m) * part + k == source, 1.0, 0.0).astype(BF), value, NN).astype(BF)


def spread(block):
    if lax.axis_size("inner") != 8 or block.shape[0] % 32:
        return {}
    return {m: swap(block, "inner", m) for m in GATHER_ORDER}


def collect(block, got):
    if not got:
        return [lax.all_gather(block, "inner", axis=0, tiled=True)]
    got = dict(got)
    got[0] = block
    for m in (0,) + GATHER_ORDER:
        got[m + 1] = swap(got[m], "inner", 1)
    return [got[m] for m in range(8)]


GATHER_ORDER = (6, 4, 2)


def pivots_from(blocks, inverse, pivots, middle, inner):
    if len(blocks) == 1:
        pivots[...] = reordered(scaled(blocks[0], inverse).astype(BF), inner, middle)
        return
    size = blocks[0].shape[0]
    part = size // middle
    made = scaled(jnp.concatenate(blocks, 0), inverse).astype(BF)
    for m in range(len(blocks)):
        at = (lax.axis_index("inner") ^ m) * part
        for q in range(middle):
            pivots[pl.ds(pl.multiple_of(q * part * inner + at, part), part), :] = (
                made[m * size + q * part:m * size + (q + 1) * part])


def up16(count):
    return (count + 15) // 16 * 16


def code_row(ref):
    return jnp.concatenate([ref[i:i + 1] for i in range(ref.shape[0])], 1)


def up16(count):
    return (count + 15) // 16 * 16


def per_device(front_leaf, front_mid, front_top, dinv_leaf, dinv_mid, dinv_top, live_rows, map_leaf, map_mid):
    rows = front_leaf.shape[0]
    panel, block = dinv_leaf.shape
    cols = front_leaf.shape[1] - panel
    inner = lax.axis_size("inner")
    half = rows // 2
    n = [cols // (inner << l) for l in range(3)]

    lanes = 128 if rows % 128 == 0 else rows
    code0 = map_leaf.reshape(rows // lanes, lanes)
    code1 = map_mid.reshape(rows // lanes, lanes)
    live = live_rows.reshape(1, 3)

    mr = dinv_mid.shape[0] // 2
    share = dinv_top.shape[0] // inner
    shared = inner == 8 and share % 16 == 0 and lanes == 128 and rows // lanes <= share and 2 * block == panel

    def pack(code0_ref, code1_ref, mid, fmid, ftop, leaf, near, c0v, c1v, head, top_head, sems):
        made = copies(sems, [
            (code0_ref, c0v), (code1_ref, c1v), (leaf.at[:n[0], :panel], head),
            (mid.at[:mr], near.at[:mr, :block]), (mid.at[mr:], near.at[:mr, block:]),
            (fmid.at[:n[1], :panel], near.at[mr + 16:mr + 16 + n[1]]), (ftop.at[:n[2], :panel], top_head),
        ])
        made[0].wait()
        code = code_row(c0v)
        parts = jnp.concatenate([code >> 8, code & 255, jnp.zeros((6, rows), I32)], 0).astype(F32).astype(BF)
        padded = jnp.concatenate([parts, jnp.zeros((8, 2 * panel - rows), BF)], 1)
        near[mr:mr + 16] = jnp.concatenate([padded[:, :panel], padded[:, panel:]], 0)
        for c in made[1:]:
            c.wait()

    near, code0, code1, block0, top_head = call(
        pack, [AN] * 6,
        [((mr + 16 + up16(n[1]), panel), BF), (code0.shape, I32), (code1.shape, I32), ((n[0], panel), BF),
         ((n[2], panel), BF)],
        scratch=[pltpu.SemaphoreType.DMA((7,))],
    )(code0, code1, dinv_mid, front_mid, front_top, front_leaf)
    got0 = spread(block0)
    near_1 = swap(near, "sub", 1)

    def sent(level):
        return [((2 * n[level] + half, cols), BF)] * 2

    def before0(live_ref, code, front, inverse, fs, cs, factor):
        pick = row_picks(code_row(code), live_ref[0:1, 0:0 + 1], n[1])
        factor[...] = factor_of(front[:, :panel], inverse[...], live_ref[0:1, 0:0 + 1])
        cs[...] = dot(pick, front[:, panel:], NN).astype(BF)
        fs[...] = dot(pick, factor[...], NN).astype(BF)

    fs0, cs0, factor0 = call(
        before0, [VM, VM, VP, VP], sent(1) + [((rows, panel), BF)],
    )(live, code0, front_leaf, dinv_leaf)
    blocks0 = collect(block0, got0)

    def chain(middle, count, headed, extra, parts):
        def body(fs, cs, inverse, *refs):
            refs = list(refs)
            head = refs.pop(0) if headed else None
            code_ref, top = (refs.pop(0), refs.pop(0)) if extra else (None, None)
            at = len(refs) - parts
            blocks, (pivots, out), bulks = refs[:at - 2], refs[at - 2:at], refs[at:]
            pivots_from([ref[...] for ref in blocks], inverse[...], pivots, middle, inner)
            used = slice(None) if parts else slice(0, 2 * count)
            update = (cs[used].astype(F32) - dot(fs[used], pivots[...], NT)).astype(BF)
            out[:count] = (update[:count].astype(F32) + head[...].astype(F32)).astype(BF) if headed else update[:count]
            out[count:2 * count] = update[count:2 * count]
            if extra:
                tail = slice(2 * count, 2 * count + share)
                at = pl.multiple_of(lax.axis_index("inner") * share, share)
                out[tail, :block] = top[pl.ds(at, share), :]
                code = jnp.concatenate([code_ref[...], jnp.zeros((share - rows // lanes, lanes), I32)], 0)
                out[tail, block:block + lanes] = (code >> 8).astype(F32).astype(BF)
                out[tail, block + lanes:] = (code & 255).astype(F32).astype(BF)
            for i, bulk in enumerate(bulks):
                bulk[...] = update[2 * count:, i * (cols // parts):(i + 1) * (cols // parts)]

        return body

    def after(level, fs, cs, inverse, blocks, parts, head=(), extra=()):
        count = n[level + 1]
        return call(
            chain(1 << level, count, bool(head), bool(extra), parts),
            [VM] * (3 + len(head) + len(extra) + len(blocks)),
            [((cols, panel), BF), ((2 * count + (share if extra else 0), cols), BF)] + [((half, cols // max(parts, 1)), BF)] * parts,
        )(fs, cs, inverse, *head, *extra, *blocks)

    def own(level, code, factor, front, pivots, parent):
        def body(live_ref, code_ref, factor_ref, front_ref, pivots_ref, parent_ref, out):
            update = (front_ref[:, panel:].astype(F32) - dot(factor_ref[...], pivots_ref[...], NT)).astype(BF)
            pick = own_pick(code_row(code_ref), live_ref[0:1, level:level + 1])
            out[...] = parent_ref[:, :cols].astype(F32) + dot(pick, update, NN)

        return call(body, [VM, VM, VM, VP, VM, VP], [((rows, cols), F32)])(
            live, code, factor, front, pivots, parent)[0]

    def rest(fs, cs, pivots, out):
        out[...] = (cs[2 * n[1]:].astype(F32) - dot(fs[2 * n[1]:], pivots[...], NT)).astype(BF)

    pivots0, pivot0 = after(0, fs0, cs0, dinv_leaf, blocks0, 0)
    bulk0, = call(rest, [VM] * 3, [((half, cols), BF)])(fs0, cs0, pivots0)
    pivot0_other = swap(pivot0, "sub", 1)
    bulk0_other = swap(bulk0, "sub", 1)

    def unpack1(mine, near_ref, inv_mid, heads1, land0):
        sub = lax.axis_index("sub")
        for q, src in enumerate((mine, near_ref)):
            at = ((sub & 1) ^ q) * 2 * mr
            inv_mid[pl.ds(pl.multiple_of(at, mr), mr), :] = src[:mr, :block]
            inv_mid[pl.ds(pl.multiple_of(at + mr, mr), mr), :] = src[:mr, block:]
            heads1[q] = src[mr + 16:]
        packed = near_ref[mr:mr + 16].astype(F32).astype(I32)
        high = jnp.concatenate([packed[0:1], packed[8:9]], 1)[:, :rows]
        low = jnp.concatenate([packed[1:2], packed[9:10]], 1)[:, :rows]
        land0[...] = landing_of(high * 256 + low, rows)

    inv_mid, heads1, land0 = call(
        unpack1, [VM] * 2,
        [(dinv_leaf.shape, BF), ((2, up16(n[1]), panel), BF), ((rows, half), BF)],
    )(near, later(near_1, pivot0))

    def early1(live_ref, code, front, pick_out, cs):
        pick = row_picks(code_row(code), live_ref[0:1, 1:1 + 1], n[2])
        pick_out[...] = pick
        cs[...] = dot(pick, front[:, panel:], NN).astype(BF)

    pick1, cs1 = call(
        early1, [VM, VM, VP], [((2 * n[2] + half, rows), BF)] + sent(2)[:1],
    )(live, later(code1, pivot0), front_mid)

    def raised(count, flip, headed, extra):
        def body(*refs):
            heads, others, out = refs[0] if headed else None, refs[headed:-1], refs[-1]
            sub = lax.axis_index("sub")

            def ordered(made):
                bit = 1
                while len(made) > 1:
                    low = (sub & bit) == 0
                    made = [
                        jnp.concatenate([jnp.where(low, a, b), jnp.where(low, b, a)], 0)
                        for a, b in zip(made[::2], made[1::2])
                    ]
                    bit *= 2
                return made[0]

            made = [
                others[q][:count].astype(F32) + others[q ^ flip][count:2 * count].astype(F32)
                for q in range(len(others))
            ]
            if headed:
                made = [heads[q][:count].astype(F32) + part for q, part in enumerate(made)]
            total = ordered(made)
            size = total.shape[0]
            out[:size] = total.astype(BF)
            if extra:
                tops = ordered([ref[2 * count:2 * count + share, :block].astype(F32) for ref in others]).astype(BF)
                for q in range(len(others)):
                    at = size + q // 2 * share
                    lane = q % 2 * block
                    out[at:at + share, lane:lane + block] = tops[q * share:(q + 1) * share]

        return body

    raw1, = call(raised(n[1], 1, 1, False), [VM] * 3, [((2 * n[1], panel), BF)])(
        later(heads1, pick1), pivot0, pivot0_other)
    spread1 = spread(raw1)
    merged0 = own(0, code0, factor0, front_leaf, pivots0, front_mid)

    def before1(live_ref, pick, merged, got, land, inverse, fs, factor):
        assembled = (merged[...] + dot(land[...], got[...], NN)).astype(BF)
        factor[...] = factor_of(assembled, inverse[...], live_ref[0:1, 1:1 + 1])
        fs[...] = dot(pick[...], factor[...], NN).astype(BF)

    fs1, factor1 = call(
        before1, [VM] * 6, sent(2)[:1] + [((rows, panel), BF)],
    )(live, pick1, merged0, bulk0_other, land0, inv_mid)
    blocks1 = collect(raw1, spread1)
    pivots1, pivot1 = after(
        1, fs1, cs1, inv_mid, blocks1, 0, (top_head,), (code1, dinv_top) if shared else ())
    others = [pivot1] + [swap(pivot1, "sub", m) for m in (1, 2, 3)]

    def rest1(fs, cs, pivots, *outs):
        for i, out in enumerate(outs):
            lane = slice(i * block, (i + 1) * block)
            out[...] = (cs[2 * n[2]:, lane].astype(F32) - dot(fs[2 * n[2]:], pivots[lane], NT)).astype(BF)

    bulk1 = call(rest1, [VM] * 3, [((half, block), BF)] * (panel // block))(fs1, cs1, pivots1)
    bulk1_other = [swap(part, "sub", 2) for part in bulk1]
    raw2, = call(raised(n[2], 2, 0, shared), [VM] * 4, [((4 * n[2] + (2 * share if shared else 0), panel), BF)])(*others)
    spread2 = spread(raw2)
    merged1 = own(1, code1, factor1, front_mid, pivots1, front_top)
    blocks2 = collect(raw2, spread2)

    def landing1(src, land1):
        if not shared:
            land1[...] = landing_of(code_row(src), rows)
            return
        packed = src[2 * n[2]:, block:].astype(F32).astype(I32)
        code = packed[:rows // lanes, :lanes] * 256 + packed[:rows // lanes, lanes:]
        land1[...] = landing_of(jnp.concatenate([code[i:i + 1] for i in range(rows // lanes)], 1), rows)

    far1 = others[2] if shared else swap(code1, "sub", 2)
    land1, = call(landing1, [VM], [((rows, half), BF)])(later(far1, raw2))

    if shared:
        def last_pivots(*refs):
            blocks, pivots, inv_top = refs[:-2], refs[-2], refs[-1]
            size = 4 * n[2]
            for m, ref in enumerate(blocks):
                for q in range(4):
                    at = q * inner * share + (lax.axis_index("inner") ^ m) * share
                    row, lane = size + q // 2 * share, q % 2 * block
                    inv_top[pl.ds(pl.multiple_of(at, share), share), :] = ref[row:row + share, lane:lane + block]
            pivots_from([ref[:size] for ref in blocks], inv_top[...], pivots, 4, inner)

        pivots2, inv_top = call(
            last_pivots, [VM] * len(blocks2), [((cols, panel), BF), (dinv_leaf.shape, BF)])(*blocks2)
    else:
        def last_pivots(inverse, *refs):
            pivots_from([ref[...] for ref in refs[:-1]], inverse[...], refs[-1], 4, inner)

        sub = lax.axis_index("sub")
        inv_top = dinv_top
        for bit in (1, 2):
            other = swap(inv_top, "sub", bit)
            inv_top = jnp.where(
                sub & bit == 0, jnp.concatenate([inv_top, other], 0), jnp.concatenate([other, inv_top], 0))
        pivots2, = call(last_pivots, [VM] * (1 + len(blocks2)), [((cols, panel), BF)])(inv_top, *blocks2)

    def level2_part(i, first, last):
        lane = slice(i * block, (i + 1) * block)

        def body(live_ref, merged, got, land, inverse, pivots, so_far, out, *scratch):
            assembled = (merged[:, lane] + dot(land[...], got[...], NN)).astype(BF)
            factor = factor_of(assembled, inverse[lane], live_ref[0:1, 2:3])
            if not last:
                out[...] = (so_far[:, panel:].astype(F32) if first else so_far[...]) - dot(factor, pivots[:, lane], NT)
                return
            ov, sems = scratch
            mask = lax.broadcasted_iota(I32, (rows, 1), 0) < live_ref[0:1, 2:3]
            writes = []
            for k in range(steps):
                at = slice(k * part, (k + 1) * part)
                start = so_far[at, panel:].astype(F32) if first else so_far[at]
                ov[at] = jnp.where(mask[at], start - dot(factor[at], pivots[:, lane], NT), 0.0).astype(BF)
                writes += copies(sems.at[k:k + 1], [(ov.at[at], out.at[at])])
            for write in writes:
                write.wait()

        return body

    steps = 2 if rows % 32 == 0 else 1
    part = rows // steps
    count = panel // block
    result = front_top
    for i in range(count):
        last = i == count - 1
        result, = call(
            level2_part(i, i == 0, last), [VM] * 6 + [VP if i == 0 else VM],
            [((rows, cols), BF if last else F32)],
            scratch=[pltpu.VMEM((rows, cols), BF), pltpu.SemaphoreType.DMA((steps,))] if last else (),
            out_specs=[AN] if last else None,
        )(live, merged1, bulk1_other[i], land1, inv_top, pivots2, result)
    return result


def solution(mesh):
    row = P(("sub", "inner"), None)
    placed = (
        row, row, row, P("sub", None), P("sub", None), P("sub", None),
        P(None, ("sub", "inner")), P(("sub", "inner")), P(("sub", "inner")),
    )

    return jax.shard_map(per_device, mesh=mesh, in_specs=placed, out_specs=row, check_vma=False)
```
